32 devices in a mesh: fsdp: 8 (over y, x, core), tp: 4 (over z).
Axes of the slice: x: 2, y: 2, z: 4, core: 2. Of those that a mesh axis runs over, the one named last changes fastest.
Arguments:
- tokens: bfloat16 [14336, 768], P(('fsdp', 'tp')), may hold values from -6 to 6
- cotangent: bfloat16 [14336, 768], P(('fsdp', 'tp')), may hold values from -6 to 6
- block_segment: int32 [112], P('fsdp'), may hold values from 0 to 6, as said below
- segment_path: int32 [56, 7], P('fsdp'), may hold values from 0 to 1, as said below
- norm1_gain: bfloat16 [768], P('fsdp'), may hold values from 0.5 to 1.5
- norm1_bias: bfloat16 [768], P('fsdp'), may hold values from -1.796875 to 1.796875
- norm2_gain: bfloat16 [768], P('fsdp'), may hold values from 0.5 to 1.5
- norm2_bias: bfloat16 [768], P('fsdp'), may hold values from -1.796875 to 1.796875
- query_weight: bfloat16 [768, 768], P('fsdp', 'tp'), may hold values from -0.21875 to 0.21875
- query_bias: bfloat16 [4, 192], P('tp', 'fsdp'), may hold values from -1.796875 to 1.796875
- kv_weight: bfloat16 [768, 128], P('fsdp'), may hold values from -0.21875 to 0.21875
- kv_bias: bfloat16 [128], P('fsdp'), may hold values from -1.796875 to 1.796875
- out_weight: bfloat16 [768, 768], P('tp', 'fsdp'), may hold values from -3.5 to 3.5
- out_bias: bfloat16 [768], P('fsdp'), may hold values from -1.796875 to 1.796875
- up_weight: bfloat16 [768, 3072], P('fsdp', 'tp'), may hold values from -0.21875 to 0.21875
- up_bias: bfloat16 [4, 768], P('tp', 'fsdp'), may hold values from -1.796875 to 1.796875
- down_weight: bfloat16 [3072, 768], P('tp', 'fsdp'), may hold values from -0.109375 to 0.109375
- down_bias: bfloat16 [768], P('fsdp'), may hold values from -1.796875 to 1.796875
Outputs:
- output: bfloat16 [14336, 768], P(('fsdp', 'tp'))
- keys_values: bfloat16 [14336, 128], P(('fsdp', 'tp'))
- input_grad: bfloat16 [14336, 768], P(('fsdp', 'tp'))
- grad_norm1_gain: float32 [768], P('fsdp')
- grad_norm1_bias: float32 [768], P('fsdp')
- grad_norm2_gain: float32 [768], P('fsdp')
- grad_norm2_bias: float32 [768], P('fsdp')
- grad_query_weight: float32 [768, 768], P('fsdp', 'tp')
- grad_query_bias: float32 [4, 192], P('tp', 'fsdp')
- grad_kv_weight: float32 [768, 128], P('fsdp')
- grad_kv_bias: float32 [128], P('fsdp')
- grad_out_weight: float32 [768, 768], P('tp', 'fsdp')
- grad_out_bias: float32 [768], P('fsdp')
- grad_up_weight: float32 [768, 3072], P('fsdp', 'tp')
- grad_up_bias: float32 [4, 768], P('tp', 'fsdp')
- grad_down_weight: float32 [3072, 768], P('tp', 'fsdp')
- grad_down_bias: float32 [768], P('fsdp')
The draws below stay inside these ranges and needn't reach their ends.
Inputs may be any that keep to these rules, and one draw needn't show every extreme that they name: `block_segment`: the 14 blocks of one index of fsdp hold one tree. A tree's 14 blocks are its trunk (8 blocks of one segment), then its 2 branches and then its 4 leaves, one block each. Tree t of its index numbers its 7 segments t * 7 to t * 7 + 6, each once, in an order drawn from the seed. `segment_path`: rows g * 7 to g * 7 + 6 are the table of index g of fsdp: entry [s, t] is 1 where segment t is s itself, the trunk of s's tree, or, for a leaf s, the branch that it grows from (each branch has exactly 2 leaves), and 0 otherwise.
All inputs are finite; a program needn't handle non-finite values.
Results may differ from the reference program's by a relative error of at most 0.013.
Values may be sent and summed in bfloat16 or wider, within the bound.
No kernel may reach another device: no remote copies, remote signals or barrier semaphores. Data moves between devices by JAX's collectives and lax.ppermute only.
A program may use at most 192 MiB of HBM per device.

```python
import math
import jax
import jax.numpy as jnp
from jax import lax

D = 768
H = 12
HD = 64
ROT = 16
FF = 3072
BLK = 128
TRUNK_BLOCKS = 8
BRANCHES = 2
LEAVES = 2
QROWS = 896
TREES_GRP = 1
GROUP = 1792
TOKENS = 14336
NBG = 14
SEGS = 7
Q_TP = 192
FF_TP = 768
N_FSDP = 8
N_TP = 4


def tree_layout(key):
    tree_total = N_FSDP * TREES_GRP
    leaf_total = BRANCHES * LEAVES
    seg_count = 1 + BRANCHES + leaf_total
    keys_all = jax.random.split(jax.random.fold_in(key, 4711), 2 * tree_total)
    labels = jax.vmap(lambda member: jax.random.permutation(member, seg_count))(keys_all[:tree_total]).astype(jnp.int32)
    parents = (jax.vmap(lambda member: jax.random.permutation(member, leaf_total))(keys_all[tree_total:]) // LEAVES).astype(jnp.int32)
    return (labels, parents, seg_count, tree_total)


def draw_block_segment(key, part):
    labels, parents, seg_count, tree_total = tree_layout(key)
    role_ids = jnp.concatenate([jnp.zeros((TRUNK_BLOCKS,), jnp.int32), 1 + jnp.arange(BRANCHES + BRANCHES * LEAVES, dtype=jnp.int32)])
    offsets = jnp.arange(tree_total, dtype=jnp.int32) % TREES_GRP * seg_count
    return (labels[:, role_ids] + offsets[:, None]).reshape(-1)


def draw_segment_path(key, part):
    labels, parents, seg_count, tree_total = tree_layout(key)
    role_ids = jnp.arange(seg_count, dtype=jnp.int32)

    def tree_table(label_row, parent_row):
        parent_role = jnp.concatenate([jnp.full((1 + BRANCHES,), -1, jnp.int32), 1 + parent_row])
        ancestry = (role_ids[None, :] == role_ids[:, None]) | (role_ids[None, :] == 0) | (role_ids[None, :] == parent_role[:, None])
        inverse = jnp.argsort(label_row)
        return ancestry.astype(jnp.int32)[inverse][:, inverse]
    tables = jax.vmap(tree_table)(labels, parents).reshape(N_FSDP, TREES_GRP, seg_count, seg_count)
    identity = jnp.eye(TREES_GRP, dtype=jnp.int32)
    return jnp.einsum('tu,gtab->gtaub', identity, tables).reshape(N_FSDP * TREES_GRP * seg_count, TREES_GRP * seg_count)


def strengthened(array, rng, source, target, parts, factor):
    def block_of(axis_at):
        return (jnp.arange(array.shape[axis_at]) // (array.shape[axis_at] // parts)).reshape((-1,) + (1,) * (array.ndim - 1 - axis_at))

    first = jax.random.permutation(rng, parts)[block_of(target)]
    second = (block_of(target) + parts // 2) % parts
    return jnp.where((block_of(source) == first) | (block_of(source) == second), factor * array, array)


def level_of(own_key, extent, pieces, smallest, high):
    def one(dim, blocks):
        draws = jax.random.uniform(jax.random.fold_in(jax.random.fold_in(own_key, 6), dim), (blocks,), jnp.float32, smallest / len(pieces), high / len(pieces))
        return jnp.repeat(jnp.exp(draws), extent[dim] // blocks).reshape((-1,) + (1,) * (len(extent) - dim - 1))

    loudness = one(*pieces[0])
    for cut in pieces[1:]:
        loudness = loudness * one(*cut)
    return loudness


def normal_values(own_key, shape, deviation, limit, cuts=(), kind=jnp.bfloat16):
    factor_of = level_of(own_key, shape, cuts, -0.22, 0.18) if cuts else 1.0
    drawn = jax.random.normal(own_key, shape, jnp.float32) * deviation * factor_of
    return jnp.minimum(jnp.maximum(drawn, -limit), limit).astype(kind)


def bell_draw_with(stream_key, extent, deviation, bound, cuts, heavy, kind=jnp.bfloat16):
    values = deviation * jax.random.normal(stream_key, extent, jnp.float32)
    if cuts:
        values = values * level_of(stream_key, extent, cuts, -0.22, 0.18)
    return jnp.clip(strengthened(values, jax.random.fold_in(stream_key, 3), *heavy), -bound, bound).astype(kind)


def setup_inputs(seed: int = 0) -> dict:
    key_of = jax.random.split(jax.random.key(seed), 19)
    return {
        "tokens": normal_values(key_of[0], (TOKENS, D), 1.0, 6.0, ((0, 32),)),
        "cotangent": bell_draw_with(key_of[1], (TOKENS, D), 1.0, 6.0, ((0, 32),), (0, 1, 32, 2.75)),
        "block_segment": draw_block_segment(jax.random.fold_in(key_of[18], 71), 0),
        "segment_path": draw_segment_path(jax.random.fold_in(key_of[18], 71), 0),
        "norm1_gain": jnp.clip(1.0 + 0.1 * jax.random.normal(key_of[4], (D,), jnp.float32), 0.5, 1.5).astype(jnp.bfloat16),
        "norm1_bias": normal_values(key_of[5], (D,), 0.3, 1.796875, ((0, 8),)),
        "norm2_gain": jnp.clip(1.0 + 0.1 * jax.random.normal(key_of[6], (D,), jnp.float32), 0.5, 1.5).astype(jnp.bfloat16),
        "norm2_bias": normal_values(key_of[7], (D,), 0.3, 1.796875, ((0, 8),)),
        "query_weight": normal_values(key_of[8], (D, H * HD), D ** -0.5, 0.21875, ((0, 8), (1, 4))),
        "query_bias": normal_values(key_of[9], (N_TP, Q_TP), 0.3, 1.796875, ((0, 4), (1, 8))),
        "kv_weight": normal_values(key_of[10], (D, 2 * HD), D ** -0.5, 0.21875, ((0, 8),)),
        "kv_bias": normal_values(key_of[11], (2 * HD,), 0.3, 1.796875, ((0, 8),)),
        "out_weight": normal_values(key_of[12], (H * HD, D), (max(1, D // 256)) ** -0.5, 3.5, ((0, 4), (1, 8))),
        "out_bias": normal_values(key_of[13], (D,), 0.3, 1.796875, ((0, 8),)),
        "up_weight": normal_values(key_of[14], (D, FF), D ** -0.5, 0.21875, ((0, 8), (1, 4))),
        "up_bias": normal_values(key_of[15], (N_TP, FF_TP), 0.3, 1.796875, ((0, 4), (1, 8))),
        "down_weight": normal_values(key_of[16], (FF, D), FF ** -0.5, 0.109375, ((0, 4), (1, 8))),
        "down_bias": normal_values(key_of[17], (D,), 0.3, 1.796875, ((0, 8),)),
    }


@jax.custom_vjp
def low(v):
    return lax.optimization_barrier(v.astype(jnp.bfloat16)).astype(jnp.float32)

@jax.custom_vjp
def low_back(v):
    return v

def low_keep(v):
    return (low(v), None)

def low_pass(kept, grad):
    return (grad,)

def back_keep(v):
    return (v, None)

def back_low(kept, grad):
    return (low(grad),)
low.defvjp(low_keep, low_pass)
low_back.defvjp(back_keep, back_low)
NORM_EPS = 1e-05
MASKED = -1000000000.0

def exact_dot(left, right):
    return jnp.dot(left, right, precision=lax.Precision.HIGHEST, preferred_element_type=jnp.float32)

def layer_norm(values, gain, shift):
    centred = values - lax.optimization_barrier(jnp.mean(values, axis=-1, keepdims=True))
    variance = lax.optimization_barrier(jnp.mean(centred * centred, axis=-1, keepdims=True))
    return centred * lax.rsqrt(variance + NORM_EPS) * gain + shift

def rotate(values, cos_table, sin_table):
    half_width = cos_table.shape[-1]
    first_half = values[..., :half_width]
    second_half = values[..., half_width:2 * half_width]
    return jnp.concatenate([first_half * cos_table - second_half * sin_table, second_half * cos_table + first_half * sin_table, values[..., 2 * half_width:]], axis=-1)

def angles(position):
    frequency = jnp.exp(jnp.arange(ROT // 2).astype(jnp.float32) * (-2.0 * math.log(10000.0) / ROT))
    phase_angle = position.astype(jnp.float32)[:, None] * frequency[None, :]
    return (jnp.cos(phase_angle), jnp.sin(phase_angle))

def group_tables(segment, path_table):
    linked = path_table[segment[:, None], segment[None, :]]
    block_count = segment.shape[0]
    earlier = jnp.arange(block_count)[:, None] > jnp.arange(block_count)[None, :]
    before = lax.optimization_barrier(jnp.sum(jnp.where(earlier, linked, 0), axis=1))
    position = (before[:, None] * BLK + jnp.arange(BLK)[None, :]).reshape(-1)
    return (linked, position)

def group_layer(inputs, linked, position, weights):
    gain_one, shift_one, gain_two, shift_two, query_mat, query_shift, kv_mat, kv_shift, out_mat, out_shift, up_mat, up_shift, down_mat, down_shift = weights
    length = inputs.shape[0]
    head_count = query_mat.shape[1] // HD
    norm_one = low(layer_norm(inputs, gain_one, shift_one))
    norm_two = low(layer_norm(inputs, gain_two, shift_two))
    cos_table, sin_table = angles(position)
    query_lin = low_back(exact_dot(norm_one, query_mat) + query_shift)
    key_value = low_back(exact_dot(norm_one, kv_mat) + kv_shift)
    query_rot = low(rotate(query_lin.reshape(length, head_count, HD), cos_table[:, None, :], sin_table[:, None, :]))
    key_rot = low(rotate(key_value[:, :HD], cos_table, sin_table))
    value_low = low(key_value[:, HD:])
    score_scale = 1.0 / math.sqrt(HD)
    key_rows = jnp.arange(length)
    key_blocks = key_rows // BLK

    def attend(member):
        query_block, query_rows = member
        raw_score = score_scale * jnp.einsum('qhd,kd->hqk', query_block, key_rot, precision=lax.Precision.HIGHEST)
        scores = low_back(raw_score)
        visible = (linked[query_rows // BLK][:, key_blocks] > 0) & (query_rows[:, None] >= key_rows[None, :])
        scores = jnp.where(visible[None], scores, MASKED)
        row_peak = lax.optimization_barrier(jnp.max(scores, axis=-1, keepdims=True))
        exponent = jnp.exp(scores - row_peak)
        probability = low(exponent / lax.optimization_barrier(jnp.sum(exponent, axis=-1, keepdims=True)))
        return jnp.einsum('hqk,kd->qhd', probability, value_low, precision=lax.Precision.HIGHEST)
    block_total = length // QROWS
    attended = lax.map(jax.checkpoint(attend), (query_rot.reshape(block_total, QROWS, head_count, HD), key_rows.reshape(block_total, QROWS)))
    attended_low = low_back(low(attended.reshape(length, head_count * HD)))
    attention_out = exact_dot(attended_low, out_mat) + out_shift
    hidden = low_back(exact_dot(norm_two, up_mat) + up_shift)
    activated = low(jax.nn.gelu(hidden, approximate=False))
    feed_forward = exact_dot(activated, down_mat) + down_shift
    return (inputs + attention_out + feed_forward, jnp.concatenate([key_rot, value_low], axis=1))

def reference(tokens, cotangent, block_segment, segment_path, norm1_gain, norm1_bias, norm2_gain, norm2_bias, query_weight, query_bias, kv_weight, kv_bias, out_weight, out_bias, up_weight, up_bias, down_weight, down_bias):
    group_total = segment_path.shape[0] // SEGS
    params = tuple((member.astype(jnp.float32) for member in (norm1_gain, norm1_bias, norm2_gain, norm2_bias, query_weight, query_bias, kv_weight, kv_bias, out_weight, out_bias, up_weight, up_bias, down_weight, down_bias)))
    link_tables, positions = jax.vmap(group_tables)(block_segment.reshape(group_total, NBG), segment_path.reshape(group_total, SEGS, SEGS))

    def layer(inputs, weights):
        flat_weights = weights[:5] + (weights[5].reshape(-1),) + weights[6:11] + (weights[11].reshape(-1),) + weights[12:]

        def one_group(member):
            return jax.checkpoint(group_layer)(member[0], member[1], member[2], flat_weights)
        result, cache = lax.map(one_group, (inputs.reshape(group_total, GROUP, D), link_tables, positions))
        return (result.reshape(-1, D), cache.reshape(-1, 2 * HD))
    (result, cache), pull_back = jax.vjp(layer, tokens.astype(jnp.float32), params)
    input_grad, weight_grads = pull_back((cotangent.astype(jnp.float32), jnp.zeros_like(cache)))
    return (result.astype(jnp.bfloat16), cache.astype(jnp.bfloat16), input_grad.astype(jnp.bfloat16), weight_grads[0], weight_grads[1], weight_grads[2], weight_grads[3], weight_grads[4], weight_grads[5], weight_grads[6], weight_grads[7], weight_grads[8], weight_grads[9], weight_grads[10], weight_grads[11], weight_grads[12], weight_grads[13])
```

```python
import functools
import math

import jax
import jax.numpy as jnp
from jax import lax
from jax.experimental import pallas as pl
from jax.experimental.pallas import tpu as pltpu
from jax.sharding import PartitionSpec as P

HD = 64
ROT = 16
BLK = 128
TRUNK = 8
FIRST_LEAF = 10
TILE = 64
HEADS_STEP = 4
CHUNKS = 3
NORM_EPS = 1e-05
MASKED = -1000000000.0
BF = jnp.bfloat16
F32 = jnp.float32


def dot(left, right, left_dim, right_dim):
    return lax.dot_general(
        left, right, (((left_dim,), (right_dim,)), ((), ())), preferred_element_type=F32
    )


def add_low(left, right):
    return (left.astype(F32) + right.astype(F32)).astype(BF)


def swap_fsdp(value, bit):
    count = lax.axis_size("fsdp")
    return lax.ppermute(value, "fsdp", [(i, i ^ bit) for i in range(count)])


def from_tp(value, step):
    count = lax.axis_size("tp")
    return lax.ppermute(value, "tp", [(i, (i - step) % count) for i in range(count)])


def core_order(mine, other, axis=0):
    core = lax.axis_index("fsdp") & 1
    return jnp.where(
        core == 0,
        jnp.concatenate([mine, other], axis=axis),
        jnp.concatenate([other, mine], axis=axis),
    )


def chip_gather(value):
    count = lax.axis_size("fsdp")
    if count == 8 and value.shape[1] % 256 == 0:
        half = value.shape[1] // 2
        near_x = swap_fsdp(value, 2)
        near_y = swap_fsdp(value, 4)
        far = jnp.concatenate(
            [swap_fsdp(near_x[:, :half], 4), swap_fsdp(near_y[:, half:], 2)], axis=1
        )
        return jnp.concatenate([value, near_x, near_y, far], axis=0)
    bit = 2
    while bit < count:
        value = jnp.concatenate([value, swap_fsdp(value, bit)], axis=0)
        bit *= 2
    return value


def chip_scatter(value):
    count = lax.axis_size("fsdp")
    rows = value.shape[0] // (count // 2)
    if count == 8 and value.shape[1] % 256 == 0:
        half = value.shape[1] // 2
        left = value[:, :half].reshape(2, 2, rows, half)
        right = value[:, half:].reshape(2, 2, rows, half)
        left = add_low(left[:, 0], swap_fsdp(left[:, 1], 2))
        right = add_low(right[0], swap_fsdp(right[1], 4))
        left = add_low(left[0], swap_fsdp(left[1], 4))
        right = add_low(right[0], swap_fsdp(right[1], 2))
        return jnp.concatenate([left, right], axis=1)
    bit = count // 2
    while bit >= 2:
        half = value.shape[0] // 2
        value = add_low(value[:half], swap_fsdp(value[half:], bit))
        bit //= 2
    return value


def tp_gather(value, axis):
    count = lax.axis_size("tp")
    return jnp.concatenate([value] + [from_tp(value, r) for r in range(1, count)], axis=axis)


def tp_scatter(value):
    count = lax.axis_size("tp")
    width = value.shape[1] // count
    total = value[:, :width].astype(F32)
    for r in range(1, count):
        total = total + from_tp(value[:, r * width : (r + 1) * width], -r).astype(F32)
    return total


def chip_relative(value, axis):
    chips = lax.axis_size("fsdp") // 2
    chip = lax.axis_index("fsdp") // 2
    size = value.shape[axis] // chips
    blocks = [lax.slice_in_dim(value, k * size, (k + 1) * size, axis=axis) for k in range(chips)]
    bit = 1
    while bit < chips:
        taken = (chip & bit) != 0
        blocks = [jnp.where(taken, blocks[k ^ bit], blocks[k]) for k in range(chips)]
        bit *= 2
    return jnp.concatenate(blocks, axis=axis)


def attention_kernel(
    meta_ref,
    query_ref,
    grad_ref,
    kv_ref,
    cos_ref,
    back_ref,
    ahead_ref,
    attended_ref,
    query_grad_ref,
    kv_grad_ref,
    queries,
    grads,
    outs,
    query_grads,
    keys,
    values,
    key_acc,
    value_acc,
    bias,
):
    step = pl.program_id(0)
    pair_count = query_ref.shape[1] // 128
    groups = queries.shape[0]
    trunk = TRUNK * BLK
    block = meta_ref[step, 0]
    offset = meta_ref[step, 1]
    parent = meta_ref[step, 2]

    @pl.when(step == 0)
    def _():
        kv_grad_ref[...] = jnp.zeros_like(kv_grad_ref)
        keys[:trunk, :] = kv_ref[:trunk, :HD]
        values[:trunk, :] = kv_ref[:trunk, HD:]

    parent_rows = pl.ds(pl.multiple_of(parent * BLK, BLK), BLK)
    own_rows = pl.ds(pl.multiple_of(block * BLK, BLK), BLK)
    keys[trunk : trunk + BLK, :] = kv_ref[parent_rows, :HD]
    values[trunk : trunk + BLK, :] = kv_ref[parent_rows, HD:]
    keys[trunk + BLK :, :] = kv_ref[own_rows, :HD]
    values[trunk + BLK :, :] = kv_ref[own_rows, HD:]

    row = lax.broadcasted_iota(jnp.int32, bias.shape, 0) + offset
    col = lax.broadcasted_iota(jnp.int32, bias.shape, 1)
    in_trunk = block < TRUNK
    trunk_limit = jnp.where(in_trunk, block * BLK + row, trunk)
    own_limit = jnp.where(in_trunk, -1, row)
    is_leaf = (block >= FIRST_LEAF).astype(jnp.int32)
    parent_limit = is_leaf * (2 * trunk) - 1
    limit = jnp.where(
        col < trunk, trunk_limit, jnp.where(col < trunk + BLK, parent_limit, own_limit + trunk + BLK)
    )
    bias[...] = jnp.where(col <= limit, 0.0, MASKED)

    cos = cos_ref[...]
    back = back_ref[...]
    ahead = ahead_ref[...]
    per_group = HEADS_STEP // 2
    for pair in range(pair_count):
        lanes = slice(pair * 128, (pair + 1) * 128)
        linear = query_ref[:, lanes]
        turned = (
            linear * cos
            + pltpu.roll(linear, 128 - ROT // 2, 1) * back
            + pltpu.roll(linear, ROT // 2, 1) * ahead
        ).astype(BF) * jnp.asarray(1.0 / math.sqrt(HD), BF)
        grad = grad_ref[:, lanes]
        group, place = divmod(pair, per_group)
        for side in range(2):
            rows = slice((2 * place + side) * TILE, (2 * place + side + 1) * TILE)
            queries[group, rows, :] = turned[:, side * HD : (side + 1) * HD]
            grads[group, rows, :] = grad[:, side * HD : (side + 1) * HD]

    key_acc[...] = jnp.zeros_like(key_acc)
    value_acc[...] = jnp.zeros_like(value_acc)

    def one_group(group, carry):
        query = queries[group]
        grad = grads[group]
        key = keys[...]
        value = values[...]
        score = dot(query, key, 1, 1)
        score = (score.reshape(HEADS_STEP, TILE, -1) + bias[...][None]).reshape(score.shape)
        peak = jnp.max(score, axis=1, keepdims=True)
        exponent = jnp.exp(score - peak)
        total = jnp.sum(exponent, axis=1, keepdims=True)
        prob = exponent * (1.0 / total)
        prob_low = prob.astype(BF)
        outs[group] = dot(prob_low, value, 1, 0)
        grad_prob = dot(grad, value, 1, 1)
        delta = jnp.sum(prob * grad_prob, axis=1, keepdims=True)
        score_grad = (prob * (grad_prob - delta)).astype(BF)
        query_grads[group] = dot(score_grad, key, 1, 0)
        key_acc[...] += dot(score_grad, query, 0, 0)
        value_acc[...] += dot(prob_low, grad, 0, 0)
        return carry

    lax.fori_loop(0, groups, one_group, 0)

    scale = 1.0 / math.sqrt(HD)
    for pair in range(pair_count):
        lanes = slice(pair * 128, (pair + 1) * 128)
        group, place = divmod(pair, per_group)
        first = slice(2 * place * TILE, (2 * place + 1) * TILE)
        second = slice((2 * place + 1) * TILE, (2 * place + 2) * TILE)
        attended_ref[:, lanes] = jnp.concatenate(
            [outs[group, first, :], outs[group, second, :]], axis=1
        ).astype(BF)
        turned = scale * jnp.concatenate(
            [query_grads[group, first, :], query_grads[group, second, :]], axis=1
        )
        query_grad_ref[:, lanes] = (
            turned * cos
            - pltpu.roll(turned, 128 - ROT // 2, 1) * back
            - pltpu.roll(turned, ROT // 2, 1) * ahead
        ).astype(BF)
    kv_grad_ref[:trunk, :HD] += key_acc[:trunk, :]
    kv_grad_ref[:trunk, HD:] += value_acc[:trunk, :]
    kv_grad_ref[parent_rows, :HD] += key_acc[trunk : trunk + BLK, :]
    kv_grad_ref[parent_rows, HD:] += value_acc[trunk : trunk + BLK, :]
    kv_grad_ref[own_rows, :HD] += key_acc[trunk + BLK :, :]
    kv_grad_ref[own_rows, HD:] += value_acc[trunk + BLK :, :]


def attention(meta, query_lin, grad_attended, key_value, cos, back, ahead):
    rows, width = query_lin.shape
    groups = width // HD // HEADS_STEP
    seen = (TRUNK + 2) * BLK
    stacked = HEADS_STEP * TILE
    tile = lambda lanes: pl.BlockSpec((TILE, lanes), lambda i, m: (i, 0))
    whole = pl.BlockSpec(key_value.shape, lambda i, m: (0, 0))
    return pl.pallas_call(
        attention_kernel,
        out_shape=(
            jax.ShapeDtypeStruct((rows, width), BF),
            jax.ShapeDtypeStruct((rows, width), BF),
            jax.ShapeDtypeStruct(key_value.shape, F32),
        ),
        grid_spec=pltpu.PrefetchScalarGridSpec(
            num_scalar_prefetch=1,
            grid=(rows // TILE,),
            in_specs=[tile(width), tile(width), whole, tile(128), tile(128), tile(128)],
            out_specs=[tile(width), tile(width), whole],
            scratch_shapes=[
                pltpu.VMEM((groups, stacked, HD), BF),
                pltpu.VMEM((groups, stacked, HD), BF),
                pltpu.VMEM((groups, stacked, HD), F32),
                pltpu.VMEM((groups, stacked, HD), F32),
                pltpu.VMEM((seen, HD), BF),
                pltpu.VMEM((seen, HD), BF),
                pltpu.VMEM((seen, HD), F32),
                pltpu.VMEM((seen, HD), F32),
                pltpu.VMEM((TILE, seen), F32),
            ],
        ),
        compiler_params=pltpu.CompilerParams(vmem_limit_bytes=40 * 2**20),
        name="tree_attention",
    )(meta, query_lin, grad_attended, key_value, cos, back, ahead)


def tree_tables(block_segment, segment_path, rank, rows):
    blocks = block_segment.shape[0]
    seg_count = segment_path.shape[1]
    one_hot = (block_segment[:, None] == jnp.arange(seg_count)[None, :]).astype(F32)
    linked = jnp.dot(jnp.dot(one_hot, segment_path.astype(F32)), one_hot.T)
    order = jnp.arange(blocks)
    before = jnp.sum(jnp.where(order[:, None] > order[None, :], linked, 0.0), axis=1)
    first_row = rank * rows
    row = first_row + jnp.arange(rows, dtype=jnp.int32)
    own = (row[:, None] // BLK == order[None, :]).astype(F32)
    position = jnp.sum(own * before[None, :], axis=1) * BLK + (row % BLK).astype(F32)
    start = first_row + TILE * jnp.arange(rows // TILE, dtype=jnp.int32)
    block = start // BLK
    second = jnp.sum((block[:, None] == order[None, :]) * linked[None, :, TRUNK + 1], axis=1)
    parent = jnp.where((block >= FIRST_LEAF) & (second > 0.5), TRUNK + 1, TRUNK)
    meta = jnp.stack([block, start % BLK, parent], axis=1).astype(jnp.int32)
    return position, meta


def body(
    tokens,
    cotangent,
    block_segment,
    segment_path,
    norm1_gain,
    norm1_bias,
    norm2_gain,
    norm2_bias,
    query_weight,
    query_bias,
    kv_weight,
    kv_bias,
    out_weight,
    out_bias,
    up_weight,
    up_bias,
    down_weight,
    down_bias,
):
    fsdp_count = lax.axis_size("fsdp")
    tp_count = lax.axis_size("tp")
    chips = fsdp_count // 2
    core = lax.axis_index("fsdp") & 1
    rank = lax.axis_index("tp")
    rows, width = tokens.shape
    shard = norm1_gain.shape[0]
    hidden_half = up_weight.shape[1] // 2
    part = hidden_half // CHUNKS

    out_turned = out_weight.T
    down_turned = down_weight.T
    keep = jnp.where(core == 0, query_weight, out_turned)
    sent = jnp.where(core == 0, out_turned, query_weight)
    attention_piece = core_order(keep, swap_fsdp(sent, 1))
    mat_kept = chip_gather(tp_gather(attention_piece, 1))

    kv_mat = core_order(kv_weight, swap_fsdp(kv_weight, 1))
    small = jnp.concatenate(
        [
            norm1_gain,
            norm1_bias,
            norm2_gain,
            norm2_bias,
            out_bias,
            down_bias,
            kv_bias,
            query_bias.reshape(-1),
            up_bias.reshape(-1),
        ]
    )[None, :]
    small = core_order(small, swap_fsdp(small, 1))
    bit = 2
    while bit < fsdp_count:
        kv_mat = jnp.concatenate([kv_mat, swap_fsdp(kv_mat, bit)], axis=0)
        small = jnp.concatenate([small, swap_fsdp(small, bit)], axis=0)
        bit *= 2
    small = small.astype(F32)
    gain_one, shift_one, gain_two, shift_two, out_shift, down_shift = (
        small[:, k * shard : (k + 1) * shard].reshape(-1) for k in range(6)
    )
    rest = chip_relative(small[:, 6 * shard :], 0)
    at = kv_bias.shape[0]
    kv_shift = rest[:, :at].reshape(-1)
    query_own = rest[:, at : at + query_bias.shape[1]].reshape(-1)
    up_own = rest[:, at + query_bias.shape[1] :].reshape(-1)
    up_own = jnp.where(core == 0, up_own[:hidden_half], up_own[hidden_half:])
    shifts = tp_gather(jnp.concatenate([query_own, up_own]).astype(BF)[None, :], 0).astype(F32)
    query_shift = shifts[:, : query_own.shape[0]].reshape(-1)
    up_shift = shifts[:, query_own.shape[0] :]

    own_half = lambda value, side: jnp.where(
        side == 0, value[:, :hidden_half], value[:, hidden_half:]
    )
    both = jnp.concatenate([own_half(up_weight, core), own_half(down_turned, core)], axis=1)
    away = jnp.concatenate([own_half(up_weight, 1 - core), own_half(down_turned, 1 - core)], axis=1)
    ffn_piece = core_order(both, swap_fsdp(away, 1))

    mat_other = swap_fsdp(mat_kept, 1)
    query_mat = jnp.where(core == 0, mat_kept, mat_other)
    out_mat = jnp.where(core == 0, mat_other, mat_kept)

    inputs = chip_relative(tokens, 1).astype(F32)
    grad_out = chip_relative(cotangent, 1)
    centred = inputs - jnp.mean(inputs, axis=-1, keepdims=True)
    inverse = lax.rsqrt(jnp.mean(centred * centred, axis=-1, keepdims=True) + NORM_EPS)
    normal = centred * inverse
    low_one = (normal * gain_one + shift_one).astype(BF)
    low_two = (normal * gain_two + shift_two).astype(BF)
    two_all = jnp.concatenate([low_two, swap_fsdp(low_two, 1)], axis=0)
    grad_all = jnp.concatenate([grad_out, swap_fsdp(grad_out, 1)], axis=0)

    position, meta = tree_tables(block_segment, segment_path, rank, rows)
    lane = jnp.arange(128, dtype=jnp.int32)
    frequency = jnp.exp((lane % (ROT // 2)).astype(F32) * (-2.0 * math.log(10000.0) / ROT))
    phase = position[:, None] * frequency[None, :]
    cos_wave = jnp.cos(phase)
    sin_wave = jnp.sin(phase)
    in_head = lane % HD
    cos = jnp.where(in_head < ROT, cos_wave, 1.0)
    back = jnp.where(in_head < ROT // 2, -sin_wave, 0.0)
    ahead = jnp.where((in_head >= ROT // 2) & (in_head < ROT), sin_wave, 0.0)
    is_key = lane < HD
    cos_key = jnp.where(is_key, cos, 1.0)
    back_key = jnp.where(is_key, back, 0.0)
    ahead_key = jnp.where(is_key, ahead, 0.0)

    kv_lin = dot(low_one, kv_mat, 1, 0) + kv_shift
    key_cache = (
        kv_lin * cos_key
        + jnp.roll(kv_lin, -(ROT // 2), 1) * back_key
        + jnp.roll(kv_lin, ROT // 2, 1) * ahead_key
    ).astype(BF)
    kv_all = jnp.zeros((rows * tp_count, key_cache.shape[1]), BF)
    for r in range(tp_count):
        piece = key_cache if r == 0 else from_tp(key_cache, r)
        kv_all = lax.dynamic_update_slice_in_dim(kv_all, piece, ((rank + r) % tp_count) * rows, 0)

    query_lin = dot(low_one, query_mat, 1, 0) + query_shift
    grad_attended = dot(grad_out, out_mat, 1, 0).astype(BF)
    attended, query_low, kv_grad = attention(
        meta, query_lin, grad_attended, kv_all, cos, back, ahead
    )
    attended_out = dot(attended, out_mat, 1, 1)
    kv_low = kv_grad.astype(BF)
    kv_sum = lax.dynamic_slice_in_dim(kv_grad, rank * rows, rows, 0)
    for r in range(1, tp_count):
        piece = lax.dynamic_slice_in_dim(kv_low, ((rank + r) % tp_count) * rows, rows, 0)
        kv_sum = kv_sum + from_tp(piece, -r).astype(F32)
    kv_low_grad = (
        kv_sum * cos_key
        - jnp.roll(kv_sum, -(ROT // 2), 1) * back_key
        - jnp.roll(kv_sum, ROT // 2, 1) * ahead_key
    ).astype(BF)
    grad_query_mat = dot(low_one, query_low, 0, 0).astype(BF)
    grad_out_mat = dot(grad_out, attended, 0, 0).astype(BF)
    grad_kv_mat = dot(low_one, kv_low_grad, 0, 0).astype(BF)
    norm_one_grad = dot(query_low, query_mat, 1, 1) + dot(kv_low_grad, kv_mat, 1, 1)

    kept = jnp.where(core == 0, grad_query_mat, grad_out_mat)
    given = jnp.where(core == 0, grad_out_mat, grad_query_mat)
    mat_sum = tp_scatter(chip_scatter(add_low(kept, swap_fsdp(given, 1))))
    mat_rows = jnp.where(core == 0, mat_sum[:shard], mat_sum[shard:])
    mat_away = swap_fsdp(jnp.where(core == 0, mat_sum[shard:], mat_sum[:shard]), 1)
    query_mat_sum = jnp.where(core == 0, mat_rows, mat_away)
    out_mat_sum = jnp.where(core == 0, mat_away, mat_rows).T

    kv_mat_part = chip_scatter(grad_kv_mat)
    kv_mat_part = add_low(
        jnp.where(core == 0, kv_mat_part[:shard], kv_mat_part[shard:]),
        swap_fsdp(jnp.where(core == 0, kv_mat_part[shard:], kv_mat_part[:shard]), 1),
    )
    kv_mat_sum = kv_mat_part.astype(F32)
    for r in range(1, tp_count):
        kv_mat_sum = kv_mat_sum + from_tp(kv_mat_part, r).astype(F32)

    branch = None
    norm_two_grad = None
    up_sums, down_sums, shift_sums = [], [], []
    for number in range(CHUNKS):
        cols = slice(number * part, (number + 1) * part)
        late = slice(hidden_half + number * part, hidden_half + (number + 1) * part)
        piece = jnp.concatenate([ffn_piece[:, cols], ffn_piece[:, late]], axis=1)
        pieces = [piece] + [from_tp(piece, r) for r in range(1, tp_count)]
        gathered = chip_gather(
            jnp.concatenate([p[:, :part] for p in pieces] + [p[:, part:] for p in pieces], axis=1)
        )
        split = part * tp_count
        up_mat = gathered[:, :split]
        down_mat = gathered[:, split:]
        hidden = dot(two_all, up_mat, 1, 0) + up_shift[:, cols].reshape(-1)
        below = 0.5 * (1.0 + lax.erf(hidden * (1.0 / math.sqrt(2.0))))
        activated = (hidden * below).astype(BF)
        slope = below + hidden * jnp.exp(-0.5 * hidden * hidden) * (1.0 / math.sqrt(2.0 * math.pi))
        hidden_low = (dot(grad_all, down_mat, 1, 0) * slope).astype(BF)
        term = dot(activated, down_mat, 1, 1)
        branch = term if branch is None else branch + term
        term = dot(hidden_low, up_mat, 1, 1)
        norm_two_grad = term if norm_two_grad is None else norm_two_grad + term
        up_grad = dot(two_all, hidden_low, 0, 0).astype(BF)
        down_grad = dot(grad_all, activated, 0, 0).astype(BF)
        shift_sums.append(jnp.sum(hidden_low.astype(F32), axis=0).reshape(tp_count, part))
        chip_sum = chip_scatter(jnp.concatenate([up_grad, down_grad], axis=1))
        parts = [
            jnp.concatenate(
                [
                    chip_sum[:, r * part : (r + 1) * part],
                    chip_sum[:, split + r * part : split + (r + 1) * part],
                ],
                axis=1,
            )
            for r in range(tp_count)
        ]
        total = parts[0].astype(F32)
        for r in range(1, tp_count):
            total = total + from_tp(parts[r], -r).astype(F32)
        own = jnp.where(core == 0, total[:shard], total[shard:])
        other = swap_fsdp(jnp.where(core == 0, total[shard:], total[:shard]), 1)
        up_sums.append((own[:, :part], other[:, :part]))
        down_sums.append((own[:, part:], other[:, part:]))

    def joined(pairs):
        return core_order(
            jnp.concatenate([p[0] for p in pairs], axis=1),
            jnp.concatenate([p[1] for p in pairs], axis=1),
            axis=1,
        )

    up_mat_sum = joined(up_sums)
    down_mat_sum = joined(down_sums).T

    branch_own = branch[:rows] + swap_fsdp(branch[rows:].astype(BF), 1).astype(F32)
    norm_two_grad = norm_two_grad[:rows] + swap_fsdp(norm_two_grad[rows:].astype(BF), 1).astype(F32)
    output = (inputs + attended_out + out_shift + branch_own + down_shift).astype(BF)
    output = chip_relative(output, 1)

    scaled = norm_one_grad * gain_one + norm_two_grad * gain_two
    input_grad = (
        grad_out.astype(F32)
        + inverse
        * (
            scaled
            - jnp.mean(scaled, axis=-1, keepdims=True)
            - normal * jnp.mean(scaled * normal, axis=-1, keepdims=True)
        )
    ).astype(BF)
    input_grad = chip_relative(input_grad, 1)

    feature_sums = chip_relative(
        jnp.stack(
            [
                jnp.sum(norm_one_grad * normal, axis=0),
                jnp.sum(norm_one_grad, axis=0),
                jnp.sum(norm_two_grad * normal, axis=0),
                jnp.sum(norm_two_grad, axis=0),
                jnp.sum(grad_out.astype(F32), axis=0),
            ]
        ),
        1,
    )
    query_sums = jnp.sum(query_low.astype(F32), axis=0).reshape(tp_count, -1)
    up_half = jnp.concatenate(shift_sums, axis=1)
    up_sums = core_order(up_half, jnp.zeros_like(up_half), axis=1)
    along = jnp.roll(jnp.concatenate([query_sums, up_sums], axis=1), rank, axis=0)
    kv_sums = jnp.sum(kv_low_grad.astype(F32), axis=0)
    vectors = jnp.concatenate([feature_sums.reshape(-1), along.reshape(-1), kv_sums])
    vectors = vectors.reshape(-1, 128)
    bit = 1
    while bit < fsdp_count:
        vectors = vectors + swap_fsdp(vectors, bit)
        bit *= 2
    total = vectors
    for r in range(1, tp_count):
        total = total + from_tp(vectors, r)
    vectors = total.reshape(-1)
    index = lax.axis_index("fsdp")
    features = vectors[: 5 * width].reshape(5, width)
    features = lax.dynamic_slice_in_dim(features, index * shard, shard, 1)
    along = vectors[5 * width : -kv_sums.shape[0]].reshape(tp_count, -1)
    along = lax.dynamic_slice_in_dim(along, rank, 1, 0)
    query_size = query_bias.shape[1]
    query_bias_sum = lax.dynamic_slice_in_dim(along, index * query_size, query_size, 1)
    up_size = up_bias.shape[1]
    up_bias_sum = lax.dynamic_slice_in_dim(
        along, query_size * fsdp_count + index * up_size, up_size, 1
    )
    kv_bias_sum = lax.dynamic_slice_in_dim(vectors[-kv_sums.shape[0] :], index * at, at, 0)
    return (
        output,
        key_cache,
        input_grad,
        features[0],
        features[1],
        features[2],
        features[3],
        query_mat_sum,
        query_bias_sum,
        kv_mat_sum,
        kv_bias_sum,
        out_mat_sum,
        features[4],
        up_mat_sum,
        up_bias_sum,
        down_mat_sum,
        features[4],
    )


def solution(mesh):
    rows = P(("fsdp", "tp"), None)
    one = P("fsdp")
    tall = P("fsdp", "tp")
    turned = P("tp", "fsdp")
    lone = P("fsdp", None)
    return jax.shard_map(
        body,
        mesh=mesh,
        in_specs=(
            *(rows, rows, one, lone, one, one, one, one, tall, turned),
            *(lone, one, turned, one, tall, turned, turned, one),
        ),
        out_specs=(
            *(rows, rows, rows, one, one, one, one, tall, turned),
            *(lone, one, turned, one, tall, turned, turned, one),
        ),
        check_vma=False,
    )
```

```python
import math

import jax
import jax.numpy as jnp
from jax import lax
from jax.experimental import pallas as pl
from jax.experimental.pallas import tpu as pltpu
from jax.sharding import PartitionSpec as P


HD = 64
ROT = 16
BLK = 128
TRUNK = 8
FIRST_LEAF = 10
TILE = 64
HEADS_STEP = 4
NORM_EPS = 1e-05
MASKED = -1000000000.0
BF = jnp.bfloat16
F32 = jnp.float32


def dot(left, right, left_dim, right_dim):
    return lax.dot_general(
        left, right, (((left_dim,), (right_dim,)), ((), ())), preferred_element_type=F32
    )


def add_low(left, right):
    return (left.astype(F32) + right.astype(F32)).astype(BF)


def swap(value, axis, bit):
    count = lax.axis_size(axis)
    return lax.ppermute(value, axis, [(i, i ^ bit) for i in range(count)])


def swap_fsdp(value, bit):
    return swap(value, "fsdp", bit)


def swap_tp(value, bit):
    return swap(value, "tp", bit)


def bits_of(count):
    return [1 << k for k in range(count.bit_length() - 1)]


def core_order(mine, other, axis=0):
    core = lax.axis_index("fsdp") & 1
    return jnp.where(
        core == 0,
        jnp.concatenate([mine, other], axis=axis),
        jnp.concatenate([other, mine], axis=axis),
    )


def direct(count):
    return count == 8


def chip_gather(value):
    count = lax.axis_size("fsdp")
    if direct(count):
        return [value] + [swap_fsdp(value, bit) for bit in (2, 4, 6)]
    for bit in bits_of(count)[1:]:
        value = jnp.concatenate([value, swap_fsdp(value, bit)], axis=0)
    return [relative(value, 0, "fsdp")]


def chip_scatter(kept, sent, bits):
    value = kept
    if sent is None:
        value = relative(kept.reshape(-1, kept.shape[2]), 0, "fsdp")
        bits = bits_of(lax.axis_size("fsdp"))[:0:-1]
        value = value.reshape(bits[0], -1, kept.shape[2])
    else:
        value = add_low(kept, swap_fsdp(sent, bits[0]))
        bits = bits[1:]
    for bit in bits:
        half = value.shape[0] // 2
        value = add_low(value[:half], swap_fsdp(value[half:], bit))
    return value[0]


def tp_gather(value, axis):
    count = lax.axis_size("tp")
    pieces = {0: value}
    for bit in reversed(bits_of(count)):
        order = sorted(pieces)
        sent = [pieces[r] for r in order]
        taken = swap_tp(sent[0] if len(sent) == 1 else jnp.concatenate(sent, axis=axis), bit)
        size = taken.shape[axis] // len(order)
        for place, r in enumerate(order):
            pieces[r | bit] = lax.slice_in_dim(taken, place * size, (place + 1) * size, axis=axis)
    return [pieces[r] for r in range(count)]


def tp_scatter(pieces, axis):
    pieces = dict(enumerate(pieces))
    bits = bits_of(len(pieces))
    for bit in bits:
        kept = [r for r in sorted(pieces) if not r & bit]
        sent = [pieces[r | bit] for r in kept]
        sent = sent[0] if len(sent) == 1 else jnp.concatenate(sent, axis=axis)
        taken = swap_tp(sent.astype(BF), bit).astype(F32)
        size = taken.shape[axis] // len(kept)
        pieces = {
            r: pieces[r].astype(F32)
            + lax.slice_in_dim(taken, place * size, (place + 1) * size, axis=axis)
            for place, r in enumerate(kept)
        }
    return pieces[0]


def tp_scatter_even(value, size):
    count = value.shape[1] // size // 2
    blocks = [value[:, k * size : (k + 1) * size] for k in range(2 * count)]
    ups, downs = blocks[:count], blocks[count:]
    for bit in reversed(bits_of(lax.axis_size("tp"))[1:]):
        count //= 2
        taken = swap_tp(jnp.concatenate(ups[count:] + downs[count:], axis=1), bit)
        taken = [taken[:, k * size : (k + 1) * size].astype(F32) for k in range(2 * count)]
        ups = [ups[k].astype(F32) + taken[k] for k in range(count)]
        downs = [downs[k].astype(F32) + taken[count + k] for k in range(count)]
    return jnp.concatenate(ups + downs, axis=1)


def relative(value, axis, name):
    count = lax.axis_size(name)
    index = lax.axis_index(name)
    if name == "fsdp":
        count, index = count // 2, index // 2
    size = value.shape[axis] // count
    blocks = [lax.slice_in_dim(value, k * size, (k + 1) * size, axis=axis) for k in range(count)]
    for bit in bits_of(count):
        taken = (index & bit) != 0
        blocks = [jnp.where(taken, blocks[k ^ bit], blocks[k]) for k in range(count)]
    return jnp.concatenate(blocks, axis=axis)


def attention_kernel(first, *refs):
    (
        meta_ref,
        query_ref,
        grad_ref,
        kv_ref,
        cos_ref,
        back_ref,
        ahead_ref,
    ) = refs[:7]
    refs = refs[7:]
    earlier = None
    if first:
        earlier = refs[2]
        refs = refs[3:]
    (
        attended_ref,
        query_grad_ref,
        kv_grad_ref,
        queries,
        grads,
        outs,
        query_grads,
        keys,
        values,
        key_acc,
        value_acc,
        bias,
    ) = refs
    step = pl.program_id(0)
    pair_count = query_ref.shape[1] // 128
    groups = queries.shape[0]
    trunk = TRUNK * BLK
    block = meta_ref[step + first, 0]
    offset = meta_ref[step + first, 1]
    parent = meta_ref[step + first, 2]

    @pl.when(step == 0)
    def _():
        if earlier is None:
            kv_grad_ref[...] = jnp.zeros_like(kv_grad_ref)
        else:
            kv_grad_ref[...] = earlier[...]
        keys[:trunk, :] = kv_ref[:trunk, :HD]
        values[:trunk, :] = kv_ref[:trunk, HD:]

    parent_rows = pl.ds(pl.multiple_of(parent * BLK, BLK), BLK)
    own_rows = pl.ds(pl.multiple_of(block * BLK, BLK), BLK)
    keys[trunk : trunk + BLK, :] = kv_ref[parent_rows, :HD]
    values[trunk : trunk + BLK, :] = kv_ref[parent_rows, HD:]
    keys[trunk + BLK :, :] = kv_ref[own_rows, :HD]
    values[trunk + BLK :, :] = kv_ref[own_rows, HD:]

    row = lax.broadcasted_iota(jnp.int32, bias.shape, 0) + offset
    col = lax.broadcasted_iota(jnp.int32, bias.shape, 1)
    in_trunk = block < TRUNK
    trunk_limit = jnp.where(in_trunk, block * BLK + row, trunk)
    own_limit = jnp.where(in_trunk, -1, row)
    is_leaf = (block >= FIRST_LEAF).astype(jnp.int32)
    parent_limit = is_leaf * (2 * trunk) - 1
    limit = jnp.where(
        col < trunk, trunk_limit, jnp.where(col < trunk + BLK, parent_limit, own_limit + trunk + BLK)
    )
    bias[...] = jnp.where(col <= limit, 0.0, MASKED)

    cos = cos_ref[...]
    back = back_ref[...]
    ahead = ahead_ref[...]
    per_group = HEADS_STEP // 2
    for pair in range(pair_count):
        lanes = slice(pair * 128, (pair + 1) * 128)
        linear = query_ref[:, lanes]
        turned = (
            linear * cos
            + pltpu.roll(linear, 128 - ROT // 2, 1) * back
            + pltpu.roll(linear, ROT // 2, 1) * ahead
        ).astype(BF) * jnp.asarray(1.0 / math.sqrt(HD), BF)
        grad = grad_ref[:, lanes]
        group, place = divmod(pair, per_group)
        for side in range(2):
            rows = slice((2 * place + side) * TILE, (2 * place + side + 1) * TILE)
            queries[group, rows, :] = turned[:, side * HD : (side + 1) * HD]
            grads[group, rows, :] = grad[:, side * HD : (side + 1) * HD]

    key_acc[...] = jnp.zeros_like(key_acc)
    value_acc[...] = jnp.zeros_like(value_acc)

    def one_group(group, carry):
        query = queries[group]
        grad = grads[group]
        key = keys[...]
        value = values[...]
        score = dot(query, key, 1, 1)
        score = (score.reshape(HEADS_STEP, TILE, -1) + bias[...][None]).reshape(score.shape)
        peak = jnp.max(score, axis=1, keepdims=True)
        exponent = jnp.exp(score - peak)
        total = jnp.sum(exponent, axis=1, keepdims=True)
        prob = exponent * (1.0 / total)
        prob_low = prob.astype(BF)
        outs[group] = dot(prob_low, value, 1, 0)
        grad_prob = dot(grad, value, 1, 1)
        delta = jnp.sum(prob * grad_prob, axis=1, keepdims=True)
        score_grad = (prob * (grad_prob - delta)).astype(BF)
        query_grads[group] = dot(score_grad, key, 1, 0)
        key_acc[...] += dot(score_grad, query, 0, 0)
        value_acc[...] += dot(prob_low, grad, 0, 0)
        return carry

    lax.fori_loop(0, groups, one_group, 0)

    scale = 1.0 / math.sqrt(HD)
    for pair in range(pair_count):
        lanes = slice(pair * 128, (pair + 1) * 128)
        group, place = divmod(pair, per_group)
        first = slice(2 * place * TILE, (2 * place + 1) * TILE)
        second = slice((2 * place + 1) * TILE, (2 * place + 2) * TILE)
        attended_ref[:, lanes] = jnp.concatenate(
            [outs[group, first, :], outs[group, second, :]], axis=1
        ).astype(BF)
        turned = scale * jnp.concatenate(
            [query_grads[group, first, :], query_grads[group, second, :]], axis=1
        )
        query_grad_ref[:, lanes] = (
            turned * cos
            - pltpu.roll(turned, 128 - ROT // 2, 1) * back
            - pltpu.roll(turned, ROT // 2, 1) * ahead
        ).astype(BF)
    kv_grad_ref[:trunk, :HD] += key_acc[:trunk, :]
    kv_grad_ref[:trunk, HD:] += value_acc[:trunk, :]
    kv_grad_ref[parent_rows, :HD] += key_acc[trunk : trunk + BLK, :]
    kv_grad_ref[parent_rows, HD:] += value_acc[trunk : trunk + BLK, :]
    kv_grad_ref[own_rows, :HD] += key_acc[trunk + BLK :, :]
    kv_grad_ref[own_rows, HD:] += value_acc[trunk + BLK :, :]


def attention(meta, query_lin, grad_attended, key_value, cos, back, ahead, first, last, earlier):
    rows, width = query_lin.shape
    groups = width // HD // HEADS_STEP
    seen = (TRUNK + 2) * BLK
    stacked = HEADS_STEP * TILE
    tile = lambda lanes: pl.BlockSpec((TILE, lanes), lambda i, m: (i + first, 0))
    whole = pl.BlockSpec(key_value.shape, lambda i, m: (0, 0))
    anywhere = pl.BlockSpec(memory_space=pl.ANY)
    given = [] if earlier is None else [anywhere, anywhere, whole]
    count = last - first
    work = 6 * count * TILE * (width // HD) * seen
    return pl.pallas_call(
        lambda *refs: attention_kernel(first, *refs),
        out_shape=(
            jax.ShapeDtypeStruct((rows, width), BF),
            jax.ShapeDtypeStruct((rows, width), BF),
            jax.ShapeDtypeStruct(key_value.shape, F32),
        ),
        grid_spec=pltpu.PrefetchScalarGridSpec(
            num_scalar_prefetch=1,
            grid=(count,),
            in_specs=[tile(width), tile(width), whole, tile(128), tile(128), tile(128)] + given,
            out_specs=[tile(width), tile(width), whole],
            scratch_shapes=[
                pltpu.VMEM((groups, stacked, HD), BF),
                pltpu.VMEM((groups, stacked, HD), BF),
                pltpu.VMEM((groups, stacked, HD), F32),
                pltpu.VMEM((groups, stacked, HD), F32),
                pltpu.VMEM((seen, HD), BF),
                pltpu.VMEM((seen, HD), BF),
                pltpu.VMEM((seen, HD), F32),
                pltpu.VMEM((seen, HD), F32),
                pltpu.VMEM((TILE, seen), F32),
            ],
        ),
        input_output_aliases={} if earlier is None else {7: 0, 8: 1},
        cost_estimate=pl.CostEstimate(
            flops=2 * 256 * work, bytes_accessed=2 * rows * width, transcendentals=work // 6
        ),
        compiler_params=pltpu.CompilerParams(vmem_limit_bytes=40 * 2**20),
    )(meta, query_lin, grad_attended, key_value, cos, back, ahead, *(earlier or ()))


def local_kernel(kernel, outs, args, scratch=(), flops=0, scalars=1):
    return pl.pallas_call(
        kernel,
        out_shape=[jax.ShapeDtypeStruct(shape, kind) for shape, kind in outs],
        in_specs=[pl.BlockSpec(memory_space=pltpu.SMEM)] * scalars
        + [pl.BlockSpec(memory_space=pltpu.VMEM)] * (len(args) - scalars),
        out_specs=[pl.BlockSpec(memory_space=pltpu.VMEM)] * len(outs),
        scratch_shapes=list(scratch),
        cost_estimate=pl.CostEstimate(flops=flops, bytes_accessed=2**20, transcendentals=0),
        compiler_params=pltpu.CompilerParams(vmem_limit_bytes=56 * 2**20),
    )(*args)


def identity(size):
    row = lax.broadcasted_iota(jnp.int32, (size, size), 0)
    col = lax.broadcasted_iota(jnp.int32, (size, size), 1)
    return jnp.where(row == col, 1.0, 0.0).astype(BF)


LINES = 16


def pack_kernel(place, query, out, up, down, kv, *refs):
    lines = refs[:-4]
    kept, sent, small, buffer = refs[-4:]
    core = place[0]
    shard, heads = query.shape
    half = up.shape[1] // 2
    unit = identity(shard)
    out_turned = dot(unit, out[...], 1, 1).astype(BF)
    down_turned = dot(unit, down[...], 1, 1).astype(BF)
    first = core == 0

    def pair(one, two, at):
        size = one.shape[1]
        one, two = one.astype(F32), two.astype(F32)
        kept[:, at : at + size] = jnp.where(first, one, two).astype(BF)
        sent[:, at : at + size] = jnp.where(first, two, one).astype(BF)

    pair(query[...], out_turned, 0)
    pair(up[:, :half], up[:, half:], heads)
    pair(down_turned[:, :half], down_turned[:, half:], heads + half)
    buffer[...] = jnp.zeros_like(buffer)
    for k, line in enumerate(lines):
        buffer[k : k + 1, : line.shape[1]] = line[...].astype(F32)
    small[:LINES, :] = buffer[...].astype(BF)
    small[LINES:, :] = kv[...]


def block_at(chip, k, size):
    return pl.ds(pl.multiple_of((chip ^ k) * size, size), size)


def place_kernel(place, *refs):
    out = refs[-1]
    for k, ref in enumerate(refs[:-1]):
        out[block_at(place[1], k, ref.shape[0]), :] = ref[...]


def send_order(bits):
    order = [0]
    for bit in reversed(bits):
        order = order + [k | bit for k in order]
    return order


def put_blocks(chip, source, kept, sent, bits):
    count = kept.shape[0] + (sent.shape[0] if sent is not None else 0)
    size = kept.shape[1]
    order = send_order(bits) if sent is not None else [0]
    for spot, k in enumerate(order):
        rows = block_at(chip, k, size) if count > 1 else slice(None)
        value = source[rows, :].astype(BF)
        if spot < kept.shape[0]:
            kept[spot] = value
        else:
            sent[spot - kept.shape[0]] = value


def mat_grad_kernel(place, one, query_low, grad, attended, kept, sent, first, second):
    core = place[0]
    first[...] = dot(one[...], query_low[...], 0, 0)
    second[...] = dot(grad[...], attended[...], 0, 0)
    count, size = kept.shape[:2]
    for k in range(count):
        rows = block_at(place[1], k, size) if count > 1 else slice(None)
        here, there = first[rows, :], second[rows, :]
        kept[k] = jnp.where(core == 0, here, there).astype(BF)
        sent[k] = jnp.where(core == 0, there, here).astype(BF)


def ffn_kernel(weight_count, sending, *refs):
    place, gain, shift, up_shift = refs[:4]
    token_refs, grad_refs = refs[4:8], refs[8:12]
    weights = refs[12 : 12 + weight_count]
    refs = refs[12 + weight_count :]
    kept, sent, sums = refs[:3]
    up_kept, down_kept = refs[3:5]
    up_sent, down_sent = refs[5:7] if sending else (None, None)
    tokens, grads, up, down, two_all, low_all, act_all, total = refs[7 if sending else 5 :]
    hidden_own = up.shape[1]
    tile = tokens.shape[1]
    pieces = tokens.shape[0]
    for k in range(4):
        for side in range(2):
            tokens[2 * k + side] = token_refs[k][side * tile : (side + 1) * tile, :]
            grads[2 * k + side] = grad_refs[k][side * tile : (side + 1) * tile, :]
    for k, ref in enumerate(weights):
        rows = block_at(place[1], k, ref.shape[0]) if weight_count > 1 else slice(None)
        up[rows, :] = ref[:, :hidden_own]
        down[rows, :] = ref[:, hidden_own:]
    sums[...] = jnp.zeros_like(sums)

    def one_tile(i, carry):
        value = tokens[i].astype(F32)
        centred = value - jnp.mean(value, axis=1, keepdims=True)
        variance = jnp.mean(centred * centred, axis=1, keepdims=True)
        normal = centred * lax.rsqrt(variance + NORM_EPS)
        two = (normal * gain[...] + shift[...]).astype(BF)
        hidden = dot(two, up[...], 1, 0) + up_shift[...]
        below = 0.5 * (1.0 + lax.erf(hidden * (1.0 / math.sqrt(2.0))))
        active = (hidden * below).astype(BF)
        bell = jnp.exp(-0.5 * hidden * hidden) * (1.0 / math.sqrt(2.0 * math.pi))
        grad = grads[i]
        slope_grad = dot(grad, down[...], 1, 0) * (below + hidden * bell)
        low = slope_grad.astype(BF)
        branch = dot(active, down[...], 1, 1)
        norm_grad = dot(low, up[...], 1, 1)
        rows = pl.ds(pl.multiple_of(i * tile, tile), tile)
        two_all[rows, :] = two
        low_all[rows, :] = low
        act_all[rows, :] = active
        sums[0:1, :] += jnp.sum(norm_grad * normal, axis=0, keepdims=True)
        sums[1:2, :] += jnp.sum(norm_grad, axis=0, keepdims=True)
        sums[2:3, :hidden_own] += jnp.sum(low.astype(F32), axis=0, keepdims=True)
        branch = branch.astype(BF)
        norm_grad = norm_grad.astype(BF)

        @pl.when(i < pieces // 2)
        def _():
            kept[0, i] = branch
            kept[1, i] = norm_grad

        @pl.when(i >= pieces // 2)
        def _():
            sent[0, i - pieces // 2] = branch
            sent[1, i - pieces // 2] = norm_grad

        return carry

    lax.fori_loop(0, pieces, one_tile, 0)
    total[...] = dot(two_all[...], low_all[...], 0, 0)
    put_blocks(place[1], total, up_kept, up_sent, (1, 2))
    flat = grads[...].reshape(act_all.shape[0], -1)
    total[...] = dot(flat, act_all[...], 0, 0)
    put_blocks(place[1], total, down_kept, down_sent, (2, 1))


def tree_tables(block_segment, segment_path, rank, rows):
    blocks = block_segment.shape[0]
    seg_count = segment_path.shape[1]
    one_hot = (block_segment[:, None] == jnp.arange(seg_count)[None, :]).astype(F32)
    linked = jnp.dot(jnp.dot(one_hot, segment_path.astype(F32)), one_hot.T)
    order = jnp.arange(blocks)
    before = jnp.sum(jnp.where(order[:, None] > order[None, :], linked, 0.0), axis=1)
    first_row = rank * rows
    row = first_row + jnp.arange(rows, dtype=jnp.int32)
    own = (row[:, None] // BLK == order[None, :]).astype(F32)
    position = jnp.sum(own * before[None, :], axis=1) * BLK + (row % BLK).astype(F32)
    start = first_row + TILE * jnp.arange(rows // TILE, dtype=jnp.int32)
    block = start // BLK
    second = jnp.sum((block[:, None] == order[None, :]) * linked[None, :, TRUNK + 1], axis=1)
    parent = jnp.where((block >= FIRST_LEAF) & (second > 0.5), TRUNK + 1, TRUNK)
    meta = jnp.stack([block, start % BLK, parent], axis=1).astype(jnp.int32)
    return position, meta


def body(
    tokens,
    cotangent,
    block_segment,
    segment_path,
    norm1_gain,
    norm1_bias,
    norm2_gain,
    norm2_bias,
    query_weight,
    query_bias,
    kv_weight,
    kv_bias,
    out_weight,
    out_bias,
    up_weight,
    up_bias,
    down_weight,
    down_bias,
):
    fsdp_count = lax.axis_size("fsdp")
    tp_count = lax.axis_size("tp")
    chips = fsdp_count // 2
    core = lax.axis_index("fsdp") & 1
    rank = lax.axis_index("tp")
    rows, width = tokens.shape
    shard = norm1_gain.shape[0]
    hidden_half = up_weight.shape[1] // 2
    heads_tp = query_weight.shape[1]
    chip = lax.axis_index("fsdp") // 2
    blocks = chips if direct(fsdp_count) else 1
    place = jnp.stack([core, chip]).astype(jnp.int32)
    pick = lambda first, second: jnp.where(core == 0, first, second)

    lines = [norm1_gain, norm1_bias, norm2_gain, norm2_bias, out_bias, down_bias, kv_bias]
    lines = [line[None, :] for line in lines] + [query_bias, up_bias]
    packed = heads_tp + 2 * hidden_half
    kept, sent, small = local_kernel(
        pack_kernel,
        [((shard, packed), BF), ((shard, packed), BF), ((LINES + shard, 128), BF)],
        [place, query_weight, out_weight, up_weight, down_weight, kv_weight, *lines],
        [pltpu.VMEM((LINES, 128), F32)],
    )
    small = small[None]
    small = core_order(small, swap_fsdp(small, 1))
    piece = core_order(kept, swap_fsdp(sent, 1))
    grad_core = swap_fsdp(cotangent, 1)
    tokens_core = swap_fsdp(tokens, 1)
    mat_piece = jnp.concatenate(tp_gather(piece[:, :heads_tp], 1), axis=1)
    mat_pieces = chip_gather(mat_piece)
    if blocks > 1:
        mat_kept = local_kernel(place_kernel, [((width, width), BF)], [place, *mat_pieces])[0]
    else:
        mat_kept = mat_pieces[0]
    mat_other = swap_fsdp(mat_kept, 1)
    query_mat = pick(mat_kept, mat_other)
    out_mat = pick(mat_other, mat_kept)

    for bit in bits_of(fsdp_count)[1:]:
        small = jnp.concatenate([small, swap_fsdp(small, bit)], axis=0)
    small = relative(small.reshape(chips, -1), 0, "fsdp").reshape(small.shape)
    kv_mat = small[:, LINES:].reshape(width, -1)
    line_at = lambda k, size: small[:, k, :size].reshape(1, -1)
    gain_one, shift_one, gain_two, shift_two, out_shift, down_shift = (
        line_at(k, shard).astype(F32) for k in range(6)
    )
    kv_shift = line_at(6, kv_bias.shape[0]).astype(F32)
    query_own = line_at(7, query_bias.shape[1])
    up_own = line_at(8, up_bias.shape[1])
    up_own = pick(up_own[:, :hidden_half], up_own[:, hidden_half:])
    shifts = jnp.concatenate(tp_gather(jnp.concatenate([query_own, up_own], axis=1), 0), axis=0)
    shifts = shifts.astype(F32)
    query_shift = shifts[:, :heads_tp].reshape(-1)
    up_shift = shifts[::2, heads_tp:].reshape(1, -1)

    inputs = tokens.astype(F32)
    centred = inputs - jnp.mean(inputs, axis=-1, keepdims=True)
    inverse = lax.rsqrt(jnp.mean(centred * centred, axis=-1, keepdims=True) + NORM_EPS)
    normal = centred * inverse
    low_one = (normal * gain_one + shift_one).astype(BF)

    ffn_piece, tokens_sent, grad_sent, _ = lax.optimization_barrier(
        (piece[:, heads_tp:], tokens, cotangent, mat_piece)
    )
    ups = [ffn_piece[:, :hidden_half]]
    downs = [ffn_piece[:, hidden_half:]]
    for bit in bits_of(tp_count)[1:]:
        near = swap_tp(jnp.concatenate(ups + downs, axis=1), bit)
        near = [near[:, k * hidden_half : (k + 1) * hidden_half] for k in range(2 * len(ups))]
        ups, downs = ups + near[: len(ups)], downs + near[len(ups) :]
    ffn_piece = jnp.concatenate(ups + downs, axis=1)
    ffn_piece, mat_pieces[-1] = lax.optimization_barrier((ffn_piece, mat_pieces[-1]))
    ffn_pieces = chip_gather(ffn_piece)
    hidden_own = hidden_half * tp_count // 2
    tokens_tp = swap_tp(tokens_sent, 1)
    grad_tp = swap_tp(grad_sent, 1)

    position, meta = tree_tables(block_segment, segment_path, rank, rows)
    lane = jnp.arange(128, dtype=jnp.int32)
    frequency = jnp.exp((lane % (ROT // 2)).astype(F32) * (-2.0 * math.log(10000.0) / ROT))
    phase = position[:, None] * frequency[None, :]
    cos_wave = jnp.cos(phase)
    sin_wave = jnp.sin(phase)
    in_head = lane % HD
    cos = jnp.where(in_head < ROT, cos_wave, 1.0)
    back = jnp.where(in_head < ROT // 2, -sin_wave, 0.0)
    ahead = jnp.where((in_head >= ROT // 2) & (in_head < ROT), sin_wave, 0.0)
    is_key = lane < HD
    cos_key = jnp.where(is_key, cos, 1.0)
    back_key = jnp.where(is_key, back, 0.0)
    ahead_key = jnp.where(is_key, ahead, 0.0)

    kv_lin = dot(low_one, kv_mat, 1, 0) + kv_shift
    key_cache = (
        kv_lin * cos_key
        + jnp.roll(kv_lin, -(ROT // 2), 1) * back_key
        + jnp.roll(kv_lin, ROT // 2, 1) * ahead_key
    ).astype(BF)
    kv_all = relative(jnp.concatenate(tp_gather(key_cache, 0), axis=0), 0, "tp")

    query_lin = dot(low_one, query_mat, 1, 0) + query_shift
    grad_attended = dot(cotangent, out_mat, 1, 0).astype(BF)
    tiles = rows // TILE
    middle = tiles * 5 // 7
    operands = (meta, query_lin, grad_attended, kv_all, cos, back, ahead)
    earlier = attention(*operands, 0, middle, None)
    tokens_tp, grad_tp, *earlier = lax.optimization_barrier((tokens_tp, grad_tp, *earlier))
    tokens_far = swap_fsdp(tokens_tp, 1)
    grad_far = swap_fsdp(grad_tp, 1)
    attended, query_low, kv_grad = attention(*operands, middle, tiles, tuple(earlier))

    first_token, attended, query_low, kv_grad = lax.optimization_barrier(
        (tokens, attended, query_low, kv_grad)
    )
    half = rows // 2
    block_rows = width // blocks
    halves = [((2, 4, half, width), BF)] * 2 + [((8, max(width, hidden_own)), F32)]
    grad_kept = [((max(blocks // 2, 1), block_rows, hidden_own), BF)] * 2
    grad_sent = grad_kept if blocks > 1 else []
    ffn_out = local_kernel(
        lambda *refs: ffn_kernel(len(ffn_pieces), blocks > 1, *refs),
        halves + grad_kept + grad_sent,
        [
            *(place, gain_two, shift_two, up_shift),
            *(first_token, tokens_tp, tokens_core, tokens_far),
            *(cotangent, grad_tp, grad_core, grad_far),
            *ffn_pieces,
        ],
        [
            pltpu.VMEM((8, half, width), BF),
            pltpu.VMEM((8, half, width), BF),
            pltpu.VMEM((width, hidden_own), BF),
            pltpu.VMEM((width, hidden_own), BF),
            pltpu.VMEM((4 * rows, width), BF),
            pltpu.VMEM((4 * rows, hidden_own), BF),
            pltpu.VMEM((4 * rows, hidden_own), BF),
            pltpu.VMEM((width, hidden_own), F32),
        ],
        flops=12 * 4 * rows * width * hidden_own,
    )
    part_kept, part_sent, ffn_vectors, up_kept, down_kept = ffn_out[:5]
    up_sent, down_sent = ffn_out[5:] if blocks > 1 else (None, None)
    part = part_kept.astype(F32) + swap_fsdp(part_sent, 1).astype(F32)
    part_tp = swap_tp(part[:, 2:].astype(BF), 1)
    up_sum = chip_scatter(up_kept, up_sent, (2, 4))
    down_sum = chip_scatter(down_kept, down_sent, (4, 2))
    ffn_sum = tp_scatter_even(jnp.concatenate([up_sum, down_sum], axis=1), hidden_half)
    ffn_own = pick(ffn_sum[:shard], ffn_sum[shard:])
    ffn_other = swap_fsdp(pick(ffn_sum[shard:], ffn_sum[:shard]), 1)
    up_mat_sum = core_order(ffn_own[:, :hidden_half], ffn_other[:, :hidden_half], axis=1)
    down_mat_sum = core_order(ffn_own[:, hidden_half:], ffn_other[:, hidden_half:], axis=1).T
    up_shift_grad = ffn_vectors[2, :hidden_own].reshape(-1, hidden_half)

    attended_out = dot(attended, out_mat, 1, 1)
    kv_pieces = relative(kv_grad, 0, "tp").reshape(tp_count, rows, -1)
    kv_sum = tp_scatter([kv_pieces[r] for r in range(tp_count)], 0)
    kv_low_grad = (
        kv_sum * cos_key
        - jnp.roll(kv_sum, -(ROT // 2), 1) * back_key
        - jnp.roll(kv_sum, ROT // 2, 1) * ahead_key
    ).astype(BF)
    mat_own, mat_given = local_kernel(
        mat_grad_kernel,
        [((blocks, block_rows, width), BF)] * 2,
        [place, low_one, query_low, cotangent, attended],
        [pltpu.VMEM((width, width), F32)] * 2,
        flops=4 * rows * width * width,
    )
    grad_kv_mat = dot(low_one, kv_low_grad, 0, 0)
    norm_one_grad = dot(query_low, query_mat, 1, 1) + dot(kv_low_grad, kv_mat, 1, 1)
    mat_own = add_low(mat_own, swap_fsdp(mat_given, 1))
    if blocks > 1:
        side = width // 2
        left = chip_scatter(mat_own[::2, :, :side], mat_own[1::2, :, :side], (2, 4))
        right = chip_scatter(mat_own[:2, :, side:], mat_own[2:, :, side:], (4, 2))
        mat_sum = jnp.concatenate([left, right], axis=1)
    else:
        mat_sum = chip_scatter(mat_own, None, None)
    mat_sum = tp_scatter(
        [mat_sum[:, r * heads_tp : (r + 1) * heads_tp] for r in range(tp_count)], 1
    )
    mat_own = pick(mat_sum[:shard], mat_sum[shard:])
    mat_away = swap_fsdp(pick(mat_sum[shard:], mat_sum[:shard]), 1)
    query_mat_sum = pick(mat_own, mat_away)
    out_mat_sum = pick(mat_away, mat_own).T

    features = jnp.stack(
        [
            jnp.sum(norm_one_grad * normal, axis=0),
            jnp.sum(norm_one_grad, axis=0),
            ffn_vectors[0, :width],
            ffn_vectors[1, :width],
            jnp.sum(cotangent.astype(F32), axis=0),
        ]
    )
    wide = lambda value: jnp.pad(value, ((0, 0), (0, 0), (0, 128 - value.shape[2])))
    features = wide(features.reshape(5, fsdp_count, shard).swapaxes(0, 1))
    query_sums = jnp.sum(query_low.astype(F32), axis=0).reshape(tp_count, -1)
    up_sums = core_order(up_shift_grad, jnp.zeros_like(up_shift_grad), axis=1)
    up_sums = jnp.stack([up_sums, jnp.zeros_like(up_sums)], axis=1).reshape(tp_count, -1)
    along = relative(jnp.concatenate([query_sums, up_sums], axis=1), 0, "tp")
    query_sums = along[:, :heads_tp].reshape(tp_count, fsdp_count, -1).swapaxes(0, 1)
    up_sums = along[:, heads_tp:].reshape(tp_count, fsdp_count, -1).swapaxes(0, 1)
    kv_sums = jnp.sum(kv_low_grad.astype(F32), axis=0).reshape(fsdp_count, 1, -1)
    vectors = jnp.concatenate(
        [
            grad_kv_mat.reshape(fsdp_count, shard, -1),
            features,
            wide(query_sums),
            wide(up_sums),
            wide(kv_sums),
        ],
        axis=1,
    )
    vectors = relative(vectors.reshape(chips, -1), 0, "fsdp").reshape(vectors.shape)
    lines = vectors.shape[1]
    vectors = vectors.reshape(chips, 2, lines, 128)
    vectors = pick(vectors[:, 0], vectors[:, 1]) + swap_fsdp(pick(vectors[:, 1], vectors[:, 0]), 1)
    for bit in reversed(bits_of(fsdp_count)[1:]):
        half = vectors.shape[0] // 2
        vectors = vectors[:half] + swap_fsdp(vectors[half:], bit)
    for bit in bits_of(tp_count):
        vectors = vectors + swap_tp(vectors, bit)
    part_tp, vectors = lax.optimization_barrier((part_tp, vectors))
    part = part[:, :2] + part_tp.astype(F32)
    branch = part[0].reshape(rows, width)
    norm_two_grad = part[1].reshape(rows, width)
    output = (inputs + attended_out + out_shift + branch + down_shift).astype(BF)
    scaled = norm_one_grad * gain_one + norm_two_grad * gain_two
    input_grad = (
        cotangent.astype(F32)
        + inverse
        * (
            scaled
            - jnp.mean(scaled, axis=-1, keepdims=True)
            - normal * jnp.mean(scaled * normal, axis=-1, keepdims=True)
        )
    ).astype(BF)

    vectors = vectors[0]
    features = vectors[shard : shard + 5, :shard]
    tail = vectors[shard + 5 :]
    query_bias_sum = lax.dynamic_slice_in_dim(tail, rank, 1, 0)[:, : query_bias.shape[1]]
    up_bias_sum = lax.dynamic_slice_in_dim(tail, tp_count + rank, 1, 0)[:, : up_bias.shape[1]]
    return (
        output,
        key_cache,
        input_grad,
        features[0],
        features[1],
        features[2],
        features[3],
        query_mat_sum,
        query_bias_sum,
        vectors[:shard],
        tail[2 * tp_count, : kv_bias.shape[0]],
        out_mat_sum,
        features[4],
        up_mat_sum,
        up_bias_sum,
        down_mat_sum,
        features[4],
    )


def solution(mesh):
    rows = P(("fsdp", "tp"), None)
    one = P("fsdp")
    tall = P("fsdp", "tp")
    turned = P("tp", "fsdp")
    lone = P("fsdp", None)
    return jax.shard_map(
        body,
        mesh=mesh,
        in_specs=(
            *(rows, rows, one, lone, one, one, one, one, tall, turned),
            *(lone, one, turned, one, tall, turned, turned, one),
        ),
        out_specs=(
            *(rows, rows, rows, one, one, one, one, tall, turned),
            *(lone, one, turned, one, tall, turned, turned, one),
        ),
        check_vma=False,
    )
```

```python
import math

import jax
import jax.numpy as jnp
from jax import lax
from jax.experimental import pallas as pl
from jax.experimental.pallas import tpu as pltpu
from jax.sharding import PartitionSpec as P


HD = 64
ROT = 16
BLK = 128
TRUNK = 8
FIRST_LEAF = 10
TILE = 64
HEADS_STEP = 4
NORM_EPS = 1e-05
MASKED = -1000000000.0
BF = jnp.bfloat16
F32 = jnp.float32


def dot(left, right, left_dim, right_dim):
    return lax.dot_general(
        left, right, (((left_dim,), (right_dim,)), ((), ())), preferred_element_type=F32
    )


def add_low(left, right):
    return (left.astype(F32) + right.astype(F32)).astype(BF)


def swap(value, axis, bit):
    count = lax.axis_size(axis)
    return lax.ppermute(value, axis, [(i, i ^ bit) for i in range(count)])


def swap_fsdp(value, bit):
    return swap(value, "fsdp", bit)


def swap_tp(value, bit):
    return swap(value, "tp", bit)


def bits_of(count):
    return [1 << k for k in range(count.bit_length() - 1)]


def core_order(mine, other, axis=0):
    core = lax.axis_index("fsdp") & 1
    return jnp.where(
        core == 0,
        jnp.concatenate([mine, other], axis=axis),
        jnp.concatenate([other, mine], axis=axis),
    )


def direct(count):
    return count == 8


def chip_gather(value):
    count = lax.axis_size("fsdp")
    if direct(count):
        return [value] + [swap_fsdp(value, bit) for bit in (2, 4, 6)]
    for bit in bits_of(count)[1:]:
        value = jnp.concatenate([value, swap_fsdp(value, bit)], axis=0)
    return [relative(value, 0, "fsdp")]


def chip_scatter(kept, sent, bits):
    value = kept
    if sent is None:
        value = relative(kept.reshape(-1, kept.shape[2]), 0, "fsdp")
        bits = bits_of(lax.axis_size("fsdp"))[:0:-1]
        value = value.reshape(bits[0], -1, kept.shape[2])
    else:
        taken = swap_fsdp(sent, bits[0])
        value = add_low(kept, taken)
        bits = bits[1:]
    for bit in bits:
        half = value.shape[0] // 2
        value = add_low(value[:half], swap_fsdp(value[half:], bit))
    return value[0]


def tp_gather(value, axis):
    count = lax.axis_size("tp")
    pieces = {0: value}
    for bit in reversed(bits_of(count)):
        order = sorted(pieces)
        sent = [pieces[r] for r in order]
        taken = swap_tp(sent[0] if len(sent) == 1 else jnp.concatenate(sent, axis=axis), bit)
        size = taken.shape[axis] // len(order)
        for place, r in enumerate(order):
            pieces[r | bit] = lax.slice_in_dim(taken, place * size, (place + 1) * size, axis=axis)
    return [pieces[r] for r in range(count)]


def tp_scatter(pieces, axis):
    pieces = dict(enumerate(pieces))
    bits = bits_of(len(pieces))
    for bit in bits:
        kept = [r for r in sorted(pieces) if not r & bit]
        sent = [pieces[r | bit] for r in kept]
        sent = sent[0] if len(sent) == 1 else jnp.concatenate(sent, axis=axis)
        taken = swap_tp(sent.astype(BF), bit).astype(F32)
        size = taken.shape[axis] // len(kept)
        pieces = {
            r: pieces[r].astype(F32)
            + lax.slice_in_dim(taken, place * size, (place + 1) * size, axis=axis)
            for place, r in enumerate(kept)
        }
    return pieces[0]


def tp_scatter_even(value, size):
    count = value.shape[1] // size // 2
    blocks = [value[:, k * size : (k + 1) * size] for k in range(2 * count)]
    ups, downs = blocks[:count], blocks[count:]
    for bit in reversed(bits_of(lax.axis_size("tp"))[1:]):
        count //= 2
        taken = swap_tp(jnp.concatenate(ups[count:] + downs[count:], axis=1), bit)
        taken = [taken[:, k * size : (k + 1) * size].astype(F32) for k in range(2 * count)]
        ups = [ups[k].astype(F32) + taken[k] for k in range(count)]
        downs = [downs[k].astype(F32) + taken[count + k] for k in range(count)]
    return jnp.concatenate(ups + downs, axis=1)


def relative(value, axis, name):
    count = lax.axis_size(name)
    index = lax.axis_index(name)
    if name == "fsdp":
        count, index = count // 2, index // 2
    size = value.shape[axis] // count
    blocks = [lax.slice_in_dim(value, k * size, (k + 1) * size, axis=axis) for k in range(count)]
    for bit in bits_of(count):
        taken = (index & bit) != 0
        blocks = [jnp.where(taken, blocks[k ^ bit], blocks[k]) for k in range(count)]
    return jnp.concatenate(blocks, axis=axis)


def attention_kernel(first, *refs):
    (
        meta_ref,
        query_ref,
        grad_ref,
        kv_ref,
        cos_ref,
        back_ref,
        ahead_ref,
    ) = refs[:7]
    refs = refs[7:]
    earlier = None
    if first:
        earlier = refs[2]
        refs = refs[3:]
    (
        attended_ref,
        query_grad_ref,
        kv_grad_ref,
        queries,
        grads,
        outs,
        query_grads,
        keys,
        values,
        acc,
        bias,
    ) = refs
    step = pl.program_id(0)
    pair_count = query_ref.shape[1] // 128
    groups = queries.shape[0]
    trunk = TRUNK * BLK
    block = meta_ref[step + first, 0]
    offset = meta_ref[step + first, 1]
    parent = meta_ref[step + first, 2]

    @pl.when(step == 0)
    def _():
        if earlier is None:
            kv_grad_ref[...] = jnp.zeros_like(kv_grad_ref)
        else:
            kv_grad_ref[...] = earlier[...]
        keys[:trunk, :] = kv_ref[:trunk, :HD]
        values[:trunk, :] = kv_ref[:trunk, HD:]

    parent_rows = pl.ds(pl.multiple_of(parent * BLK, BLK), BLK)
    own_rows = pl.ds(pl.multiple_of(block * BLK, BLK), BLK)
    keys[trunk : trunk + BLK, :] = kv_ref[parent_rows, :HD]
    values[trunk : trunk + BLK, :] = kv_ref[parent_rows, HD:]
    keys[trunk + BLK :, :] = kv_ref[own_rows, :HD]
    values[trunk + BLK :, :] = kv_ref[own_rows, HD:]

    row = lax.broadcasted_iota(jnp.int32, bias.shape, 0) + offset
    col = lax.broadcasted_iota(jnp.int32, bias.shape, 1)
    in_trunk = block < TRUNK
    trunk_limit = jnp.where(in_trunk, block * BLK + row, trunk)
    own_limit = jnp.where(in_trunk, -1, row)
    is_leaf = (block >= FIRST_LEAF).astype(jnp.int32)
    parent_limit = is_leaf * (2 * trunk) - 1
    limit = jnp.where(
        col < trunk, trunk_limit, jnp.where(col < trunk + BLK, parent_limit, own_limit + trunk + BLK)
    )
    bias[...] = jnp.where(col <= limit, 0.0, MASKED)

    cos = cos_ref[...]
    back = back_ref[...]
    ahead = ahead_ref[...]
    per_group = HEADS_STEP // 2
    for pair in range(pair_count):
        lanes = slice(pair * 128, (pair + 1) * 128)
        linear = query_ref[:, lanes]
        turned = (
            linear * cos
            + pltpu.roll(linear, 128 - ROT // 2, 1) * back
            + pltpu.roll(linear, ROT // 2, 1) * ahead
        ).astype(BF) * jnp.asarray(1.0 / math.sqrt(HD), BF)
        grad = grad_ref[:, lanes]
        group, place = divmod(pair, per_group)
        for side in range(2):
            rows = slice((2 * place + side) * TILE, (2 * place + side + 1) * TILE)
            queries[group, rows, :] = turned[:, side * HD : (side + 1) * HD]
            grads[group, rows, :] = grad[:, side * HD : (side + 1) * HD]

    acc[...] = jnp.zeros_like(acc)

    def one_group(group, carry):
        query = queries[group]
        grad = grads[group]
        key = keys[...]
        value = values[...]
        score = dot(query, key, 1, 1)
        score = (score.reshape(HEADS_STEP, TILE, -1) + bias[...][None]).reshape(score.shape)
        peak = jnp.max(score, axis=1, keepdims=True)
        exponent = jnp.exp(score - peak)
        total = jnp.sum(exponent, axis=1, keepdims=True)
        prob = exponent * (1.0 / total)
        prob_low = prob.astype(BF)
        outs[group] = dot(prob_low, value, 1, 0)
        grad_prob = dot(grad, value, 1, 1)
        delta = jnp.sum(prob * grad_prob, axis=1, keepdims=True)
        score_grad = (prob * (grad_prob - delta)).astype(BF)
        query_grads[group] = dot(score_grad, key, 1, 0)
        acc[:HD, :] += dot(query, score_grad, 0, 0)
        acc[HD:, :] += dot(grad, prob_low, 0, 0)
        return carry

    lax.fori_loop(0, groups, one_group, 0)

    scale = 1.0 / math.sqrt(HD)
    for pair in range(pair_count):
        lanes = slice(pair * 128, (pair + 1) * 128)
        group, place = divmod(pair, per_group)
        first = slice(2 * place * TILE, (2 * place + 1) * TILE)
        second = slice((2 * place + 1) * TILE, (2 * place + 2) * TILE)
        attended_ref[:, lanes] = jnp.concatenate(
            [outs[group, first, :], outs[group, second, :]], axis=1
        ).astype(BF)
        turned = scale * jnp.concatenate(
            [query_grads[group, first, :], query_grads[group, second, :]], axis=1
        )
        query_grad_ref[:, lanes] = (
            turned * cos
            - pltpu.roll(turned, 128 - ROT // 2, 1) * back
            - pltpu.roll(turned, ROT // 2, 1) * ahead
        ).astype(BF)
    kv_grad_ref[:, :trunk] += acc[:, :trunk]
    kv_grad_ref[:, parent_rows] += acc[:, trunk : trunk + BLK]
    kv_grad_ref[:, own_rows] += acc[:, trunk + BLK :]


def attention(meta, query_lin, grad_attended, key_value, cos, back, ahead, first, last, earlier):
    rows, width = query_lin.shape
    groups = width // HD // HEADS_STEP
    seen = (TRUNK + 2) * BLK
    stacked = HEADS_STEP * TILE
    tile = lambda lanes: pl.BlockSpec((TILE, lanes), lambda i, m: (i + first, 0))
    whole = pl.BlockSpec(key_value.shape, lambda i, m: (0, 0))
    anywhere = pl.BlockSpec(memory_space=pl.ANY)
    turned = pl.BlockSpec(key_value.shape[::-1], lambda i, m: (0, 0))
    given = [] if earlier is None else [anywhere, anywhere, turned]
    count = last - first
    work = 6 * count * TILE * (width // HD) * seen
    return pl.pallas_call(
        lambda *refs: attention_kernel(first, *refs),
        out_shape=(
            jax.ShapeDtypeStruct((rows, width), BF),
            jax.ShapeDtypeStruct((rows, width), BF),
            jax.ShapeDtypeStruct(key_value.shape[::-1], F32),
        ),
        grid_spec=pltpu.PrefetchScalarGridSpec(
            num_scalar_prefetch=1,
            grid=(count,),
            in_specs=[tile(width), tile(width), whole, tile(128), tile(128), tile(128)] + given,
            out_specs=[tile(width), tile(width), turned],
            scratch_shapes=[
                pltpu.VMEM((groups, stacked, HD), BF),
                pltpu.VMEM((groups, stacked, HD), BF),
                pltpu.VMEM((groups, stacked, HD), F32),
                pltpu.VMEM((groups, stacked, HD), F32),
                pltpu.VMEM((seen, HD), BF),
                pltpu.VMEM((seen, HD), BF),
                pltpu.VMEM((2 * HD, seen), F32),
                pltpu.VMEM((TILE, seen), F32),
            ],
        ),
        input_output_aliases={} if earlier is None else {7: 0, 8: 1},
        cost_estimate=pl.CostEstimate(
            flops=2 * 256 * work, bytes_accessed=2 * rows * width, transcendentals=work // 6
        ),
        compiler_params=pltpu.CompilerParams(vmem_limit_bytes=40 * 2**20),
    )(meta, query_lin, grad_attended, key_value, cos, back, ahead, *(earlier or ()))


def local_kernel(kernel, outs, args, scratch=(), flops=0, scalars=1):
    return pl.pallas_call(
        kernel,
        out_shape=[jax.ShapeDtypeStruct(shape, kind) for shape, kind in outs],
        in_specs=[pl.BlockSpec(memory_space=pltpu.SMEM)] * scalars
        + [pl.BlockSpec(memory_space=pltpu.VMEM)] * (len(args) - scalars),
        out_specs=[pl.BlockSpec(memory_space=pltpu.VMEM)] * len(outs),
        scratch_shapes=list(scratch),
        cost_estimate=pl.CostEstimate(flops=flops, bytes_accessed=2**20, transcendentals=0),
        compiler_params=pltpu.CompilerParams(vmem_limit_bytes=56 * 2**20),
    )(*args)


def identity(size):
    row = lax.broadcasted_iota(jnp.int32, (size, size), 0)
    col = lax.broadcasted_iota(jnp.int32, (size, size), 1)
    return jnp.where(row == col, 1.0, 0.0).astype(BF)


LINES = 16


def pack_kernel(place, query, out, up, down, kv, *refs):
    lines = refs[:-4]
    kept, sent, small, buffer = refs[-4:]
    core = place[0]
    shard, heads = query.shape
    half = up.shape[1] // 2
    unit = identity(shard)
    out_turned = dot(unit, out[...], 1, 1).astype(BF)
    down_turned = down[...]
    first = core == 0

    def pair(one, two, at):
        size = one.shape[1]
        one, two = one.astype(F32), two.astype(F32)
        kept[:, at : at + size] = jnp.where(first, one, two).astype(BF)
        sent[:, at : at + size] = jnp.where(first, two, one).astype(BF)

    pair(query[...], out_turned, 0)
    pair(up[:, :half], up[:, half:], heads)
    pair(down_turned[:, :half], down_turned[:, half:], heads + half)
    buffer[...] = jnp.zeros_like(buffer)
    for k, line in enumerate(lines):
        buffer[k : k + 1, : line.shape[1]] = line[...].astype(F32)
    small[:LINES, :] = buffer[...].astype(BF)
    small[LINES:, :] = kv[...]


def block_at(chip, k, size):
    return pl.ds(pl.multiple_of((chip ^ k) * size, size), size)


def place_kernel(place, *refs):
    out = refs[-1]
    for k, ref in enumerate(refs[:-1]):
        out[block_at(place[1], k, ref.shape[0]), :] = ref[...]


def send_order(bits):
    order = [0]
    for bit in reversed(bits):
        order = order + [k | bit for k in order]
    return order


def put_blocks(chip, source, kept, sent, bits):
    count = kept.shape[0] + (sent.shape[0] if sent is not None else 0)
    size = kept.shape[1]
    order = send_order(bits) if sent is not None else [0]
    for spot, k in enumerate(order):
        rows = block_at(chip, k, size) if count > 1 else slice(None)
        value = source[rows, :].astype(BF)
        if spot < kept.shape[0]:
            kept[spot] = value
        else:
            sent[spot - kept.shape[0]] = value


def finish_kernel(
    kept, taken, from_pair, tokens, grad, base, one_grad, gain_one, gain_two, shift, out, input_grad
):
    part = kept[:, 0].astype(F32) + taken[:, 0].astype(F32) + from_pair[:, 0].astype(F32)
    value = tokens[...].astype(F32)
    out[...] = (value + base[...] + shift[...] + part[0]).astype(BF)
    centred = value - jnp.mean(value, axis=1, keepdims=True)
    inverse = lax.rsqrt(jnp.mean(centred * centred, axis=1, keepdims=True) + NORM_EPS)
    normal = centred * inverse
    scaled = one_grad[...] * gain_one[...] + part[1] * gain_two[...]
    mean = jnp.mean(scaled, axis=1, keepdims=True)
    along = jnp.mean(scaled * normal, axis=1, keepdims=True)
    input_grad[...] = (
        grad[...].astype(F32) + inverse * (scaled - mean - normal * along)
    ).astype(BF)


def finish(kept, taken, from_pair, tokens, grad, base, one_grad, gain_one, gain_two, shift):
    rows, width = tokens.shape
    half = kept.shape[2]
    parts = pl.BlockSpec((2, 1, half, width), lambda i: (0, i, 0, 0))
    tile = pl.BlockSpec((half, width), lambda i: (i, 0))
    line = pl.BlockSpec((1, width), lambda i: (0, 0))
    call = pl.pallas_call(
        finish_kernel,
        grid=(rows // half,),
        out_shape=[jax.ShapeDtypeStruct((rows, width), BF)] * 2,
        in_specs=[parts] * 3 + [tile] * 4 + [line] * 3,
        out_specs=[tile] * 2,
        cost_estimate=pl.CostEstimate(
            flops=30 * rows * width, bytes_accessed=24 * rows * width, transcendentals=0
        ),
        name="finish",
    )
    return call(
        kept, taken, from_pair, tokens, grad, base, one_grad, gain_one, gain_two, shift
    )


def mat_grad_kernel(place, one, query_low, grad, attended, kept, sent, first, second):
    core = place[0]
    first[...] = dot(one[...], query_low[...], 0, 0)
    second[...] = dot(grad[...], attended[...], 0, 0)
    count, size = kept.shape[:2]
    for k in range(count):
        rows = block_at(place[1], k, size) if count > 1 else slice(None)
        here, there = first[rows, :], second[rows, :]
        kept[k] = jnp.where(core == 0, here, there).astype(BF)
        sent[k] = jnp.where(core == 0, there, here).astype(BF)


def ffn_kernel(weight_count, sending, *refs):
    place, gain, shift, up_shift = refs[:4]
    token_refs, grad_refs = refs[4:8], refs[8:12]
    weights = refs[12 : 12 + weight_count]
    refs = refs[12 + weight_count :]
    kept, sent, sums = refs[:3]
    up_kept, down_kept = refs[3:5]
    up_sent, down_sent = refs[5:7] if sending else (None, None)
    tokens, grads, up, down, two_all, low_all, act_all, total = refs[7 if sending else 5 :]
    hidden_own = up.shape[1]
    tile = tokens.shape[1]
    pieces = tokens.shape[0]
    for k in range(4):
        for side in range(2):
            tokens[2 * k + side] = token_refs[k][side * tile : (side + 1) * tile, :]
            grads[2 * k + side] = grad_refs[k][side * tile : (side + 1) * tile, :]
    for k, ref in enumerate(weights):
        rows = block_at(place[1], k, ref.shape[0]) if weight_count > 1 else slice(None)
        up[rows, :] = ref[:, :hidden_own]
        down[rows, :] = ref[:, hidden_own:]
    sums[...] = jnp.zeros_like(sums)

    def one_tile(i, carry):
        value = tokens[i].astype(F32)
        centred = value - jnp.mean(value, axis=1, keepdims=True)
        variance = jnp.mean(centred * centred, axis=1, keepdims=True)
        normal = centred * lax.rsqrt(variance + NORM_EPS)
        two = (normal * gain[...] + shift[...]).astype(BF)
        hidden = dot(two, up[...], 1, 0) + up_shift[...]
        below = 0.5 * (1.0 + lax.erf(hidden * (1.0 / math.sqrt(2.0))))
        active = (hidden * below).astype(BF)
        bell = jnp.exp(-0.5 * hidden * hidden) * (1.0 / math.sqrt(2.0 * math.pi))
        grad = grads[i]
        slope_grad = dot(grad, down[...], 1, 0) * (below + hidden * bell)
        low = slope_grad.astype(BF)
        branch = dot(active, down[...], 1, 1)
        norm_grad = dot(low, up[...], 1, 1)
        rows = pl.ds(pl.multiple_of(i * tile, tile), tile)
        two_all[rows, :] = two
        low_all[rows, :] = low
        act_all[rows, :] = active
        sums[0:1, :] += jnp.sum(norm_grad * normal, axis=0, keepdims=True)
        sums[1:2, :] += jnp.sum(norm_grad, axis=0, keepdims=True)
        sums[2:3, :hidden_own] += jnp.sum(low.astype(F32), axis=0, keepdims=True)
        branch = branch.astype(BF)
        norm_grad = norm_grad.astype(BF)

        @pl.when(i < pieces // 2)
        def _():
            kept[0, i] = branch
            kept[1, i] = norm_grad

        @pl.when(i >= pieces // 2)
        def _():
            sent[0, i - pieces // 2] = branch
            sent[1, i - pieces // 2] = norm_grad

        return carry

    lax.fori_loop(0, pieces, one_tile, 0)
    total[...] = dot(two_all[...], low_all[...], 0, 0)
    put_blocks(place[1], total, up_kept, up_sent, (1, 2))
    flat = grads[...].reshape(act_all.shape[0], -1)
    total[...] = dot(flat, act_all[...], 0, 0)
    put_blocks(place[1], total, down_kept, down_sent, (2, 1))


def tree_tables(block_segment, segment_path, rank, rows):
    blocks = block_segment.shape[0]
    seg_count = segment_path.shape[1]
    one_hot = (block_segment[:, None] == jnp.arange(seg_count)[None, :]).astype(F32)
    linked = jnp.dot(jnp.dot(one_hot, segment_path.astype(F32)), one_hot.T)
    order = jnp.arange(blocks)
    before = jnp.sum(jnp.where(order[:, None] > order[None, :], linked, 0.0), axis=1)
    first_row = rank * rows
    row = first_row + jnp.arange(rows, dtype=jnp.int32)
    own = (row[:, None] // BLK == order[None, :]).astype(F32)
    position = jnp.sum(own * before[None, :], axis=1) * BLK + (row % BLK).astype(F32)
    start = first_row + TILE * jnp.arange(rows // TILE, dtype=jnp.int32)
    block = start // BLK
    second = jnp.sum((block[:, None] == order[None, :]) * linked[None, :, TRUNK + 1], axis=1)
    parent = jnp.where((block >= FIRST_LEAF) & (second > 0.5), TRUNK + 1, TRUNK)
    meta = jnp.stack([block, start % BLK, parent], axis=1).astype(jnp.int32)
    return position, meta


def body(
    tokens,
    cotangent,
    block_segment,
    segment_path,
    norm1_gain,
    norm1_bias,
    norm2_gain,
    norm2_bias,
    query_weight,
    query_bias,
    kv_weight,
    kv_bias,
    out_weight,
    out_bias,
    up_weight,
    up_bias,
    down_weight,
    down_bias,
):
    fsdp_count = lax.axis_size("fsdp")
    tp_count = lax.axis_size("tp")
    chips = fsdp_count // 2
    core = lax.axis_index("fsdp") & 1
    rank = lax.axis_index("tp")
    rows, width = tokens.shape
    shard = norm1_gain.shape[0]
    hidden_half = up_weight.shape[1] // 2
    heads_tp = query_weight.shape[1]
    chip = lax.axis_index("fsdp") // 2
    blocks = chips if direct(fsdp_count) else 1
    place = jnp.stack([core, chip]).astype(jnp.int32)
    pick = lambda first, second: jnp.where(core == 0, first, second)

    lines = [norm1_gain, norm1_bias, norm2_gain, norm2_bias, out_bias, down_bias, kv_bias]
    lines = [line[None, :] for line in lines] + [query_bias, up_bias]
    packed = heads_tp + 2 * hidden_half
    kept, sent, small = local_kernel(
        pack_kernel,
        [((shard, packed), BF), ((shard, packed), BF), ((LINES + shard, 128), BF)],
        [place, query_weight, out_weight, up_weight, down_weight.T, kv_weight, *lines],
        [pltpu.VMEM((LINES, 128), F32)],
    )
    small = small[None]
    small = core_order(small, swap_fsdp(small, 1))
    piece = core_order(kept, swap_fsdp(sent, 1))
    grad_core = swap_fsdp(cotangent, 1)
    tokens_core = swap_fsdp(tokens, 1)
    mat_piece = jnp.concatenate(tp_gather(piece[:, :heads_tp], 1), axis=1)
    mat_pieces = chip_gather(mat_piece)
    if blocks > 1:
        mat_kept = local_kernel(place_kernel, [((width, width), BF)], [place, *mat_pieces])[0]
    else:
        mat_kept = mat_pieces[0]
    mat_other = swap_fsdp(mat_kept, 1)
    query_mat = pick(mat_kept, mat_other)
    out_mat = pick(mat_other, mat_kept)

    for bit in bits_of(fsdp_count)[1:]:
        small = jnp.concatenate([small, swap_fsdp(small, bit)], axis=0)
    small = relative(small.reshape(chips, -1), 0, "fsdp").reshape(small.shape)
    kv_mat = small[:, LINES:].reshape(width, -1)
    line_at = lambda k, size: small[:, k, :size].reshape(1, -1)
    gain_one, shift_one, gain_two, shift_two, out_shift, down_shift = (
        line_at(k, shard).astype(F32) for k in range(6)
    )
    kv_shift = line_at(6, kv_bias.shape[0]).astype(F32)
    query_own = line_at(7, query_bias.shape[1])
    up_own = line_at(8, up_bias.shape[1])
    up_own = pick(up_own[:, :hidden_half], up_own[:, hidden_half:])
    shift_own = jnp.concatenate([query_own, up_own], axis=1)
    shift_size = shift_own.shape[1]
    shift_own = jnp.pad(shift_own, ((0, 0), (0, -shift_size % 2048))).reshape(-1, 128)

    inputs = tokens.astype(F32)
    centred = inputs - jnp.mean(inputs, axis=-1, keepdims=True)
    inverse = lax.rsqrt(jnp.mean(centred * centred, axis=-1, keepdims=True) + NORM_EPS)
    normal = centred * inverse
    low_one = (normal * gain_one + shift_one).astype(BF)

    ffn_piece, tokens_sent, grad_sent, _ = lax.optimization_barrier(
        (piece[:, heads_tp:], tokens, cotangent, mat_piece)
    )
    ups = [ffn_piece[:, :hidden_half]]
    downs = [ffn_piece[:, hidden_half:]]
    for bit in bits_of(tp_count)[1:]:
        near = swap_tp(jnp.concatenate(ups + downs, axis=1), bit)
        near = [near[:, k * hidden_half : (k + 1) * hidden_half] for k in range(2 * len(ups))]
        ups, downs = ups + near[: len(ups)], downs + near[len(ups) :]
    ffn_piece = jnp.concatenate(ups + downs, axis=1)
    ffn_piece, mat_pieces[-1] = lax.optimization_barrier((ffn_piece, mat_pieces[-1]))
    ffn_pieces = chip_gather(ffn_piece)
    hidden_own = hidden_half * tp_count // 2
    tokens_tp = swap_tp(tokens_sent, 1)
    grad_tp = swap_tp(grad_sent, 1)

    position, meta = tree_tables(block_segment, segment_path, rank, rows)
    lane = jnp.arange(128, dtype=jnp.int32)
    frequency = jnp.exp((lane % (ROT // 2)).astype(F32) * (-2.0 * math.log(10000.0) / ROT))
    phase = position[:, None] * frequency[None, :]
    cos_wave = jnp.cos(phase)
    sin_wave = jnp.sin(phase)
    in_head = lane % HD
    cos = jnp.where(in_head < ROT, cos_wave, 1.0)
    back = jnp.where(in_head < ROT // 2, -sin_wave, 0.0)
    ahead = jnp.where((in_head >= ROT // 2) & (in_head < ROT), sin_wave, 0.0)
    is_key = lane < HD
    cos_key = jnp.where(is_key, cos, 1.0)
    back_key = jnp.where(is_key, back, 0.0)
    ahead_key = jnp.where(is_key, ahead, 0.0)

    kv_lin = dot(low_one, kv_mat, 1, 0) + kv_shift
    key_cache = (
        kv_lin * cos_key
        + jnp.roll(kv_lin, -(ROT // 2), 1) * back_key
        + jnp.roll(kv_lin, ROT // 2, 1) * ahead_key
    ).astype(BF)
    gathered = tp_gather(jnp.concatenate([key_cache, shift_own], axis=0), 0)
    kv_all = relative(jnp.concatenate([g[:rows] for g in gathered], axis=0), 0, "tp")
    shifts = jnp.concatenate(
        [g[rows:].reshape(1, -1)[:, :shift_size] for g in gathered], axis=0
    ).astype(F32)
    query_shift = shifts[:, :heads_tp].reshape(-1)
    up_shift = shifts[::2, heads_tp:].reshape(1, -1)

    query_lin = dot(low_one, query_mat, 1, 0) + query_shift
    grad_attended = dot(cotangent, out_mat, 1, 0).astype(BF)
    tiles = rows // TILE
    middle = tiles * 5 // 7
    operands = (meta, query_lin, grad_attended, kv_all, cos, back, ahead)
    earlier = attention(*operands, 0, middle, None)
    tokens_tp, grad_tp, *earlier = lax.optimization_barrier((tokens_tp, grad_tp, *earlier))
    tokens_far = swap_fsdp(tokens_tp, 1)
    grad_far = swap_fsdp(grad_tp, 1)
    attended, query_low, kv_grad = attention(*operands, middle, tiles, tuple(earlier))

    first_token, attended, query_low, kv_grad = lax.optimization_barrier(
        (tokens, attended, query_low, kv_grad)
    )
    half = rows // 2
    block_rows = width // blocks
    halves = [((2, 4, half, width), BF)] * 2 + [((8, max(width, hidden_own)), F32)]
    grad_kept = [((max(blocks // 2, 1), block_rows, hidden_own), BF)] * 2
    grad_sent = grad_kept if blocks > 1 else []
    ffn_out = local_kernel(
        lambda *refs: ffn_kernel(len(ffn_pieces), blocks > 1, *refs),
        halves + grad_kept + grad_sent,
        [
            *(place, gain_two, shift_two, up_shift),
            *(first_token, tokens_tp, tokens_core, tokens_far),
            *(cotangent, grad_tp, grad_core, grad_far),
            *ffn_pieces,
        ],
        [
            pltpu.VMEM((8, half, width), BF),
            pltpu.VMEM((8, half, width), BF),
            pltpu.VMEM((width, hidden_own), BF),
            pltpu.VMEM((width, hidden_own), BF),
            pltpu.VMEM((4 * rows, width), BF),
            pltpu.VMEM((4 * rows, hidden_own), BF),
            pltpu.VMEM((4 * rows, hidden_own), BF),
            pltpu.VMEM((width, hidden_own), F32),
        ],
        flops=12 * 4 * rows * width * hidden_own,
    )
    part_kept, part_sent, ffn_vectors, up_kept, down_kept = ffn_out[:5]
    up_sent, down_sent = ffn_out[5:] if blocks > 1 else (None, None)
    part_core = swap_fsdp(part_sent, 1)
    part_tp = swap_tp(add_low(part_kept[:, 2:], part_core[:, 2:]), 1)
    up_sum = chip_scatter(up_kept, up_sent, (2, 4))
    down_sum = chip_scatter(down_kept, down_sent, (4, 2))
    ffn_sum = tp_scatter_even(jnp.concatenate([up_sum, down_sum], axis=1), hidden_half)
    ffn_own = pick(ffn_sum[:shard], ffn_sum[shard:])
    ffn_other = swap_fsdp(pick(ffn_sum[shard:], ffn_sum[:shard]), 1)
    up_mat_sum = core_order(ffn_own[:, :hidden_half], ffn_other[:, :hidden_half], axis=1)
    down_mat_sum = core_order(ffn_own[:, hidden_half:], ffn_other[:, hidden_half:], axis=1).T
    up_shift_grad = ffn_vectors[2, :hidden_own].reshape(-1, hidden_half)

    attended_out = dot(attended, out_mat, 1, 1)
    kv_pieces = relative(kv_grad.T, 0, "tp").reshape(tp_count, rows, -1)
    kv_sum = tp_scatter([kv_pieces[r] for r in range(tp_count)], 0)
    kv_low_grad = (
        kv_sum * cos_key
        - jnp.roll(kv_sum, -(ROT // 2), 1) * back_key
        - jnp.roll(kv_sum, ROT // 2, 1) * ahead_key
    ).astype(BF)
    mat_own, mat_given = local_kernel(
        mat_grad_kernel,
        [((blocks, block_rows, width), BF)] * 2,
        [place, low_one, query_low, cotangent, attended],
        [pltpu.VMEM((width, width), F32)] * 2,
        flops=4 * rows * width * width,
    )
    grad_kv_mat = dot(low_one, kv_low_grad, 0, 0)
    norm_one_grad = dot(query_low, query_mat, 1, 1) + dot(kv_low_grad, kv_mat, 1, 1)
    mat_own = add_low(mat_own, swap_fsdp(mat_given, 1))
    if blocks > 1:
        side = width // 2
        left = chip_scatter(mat_own[::2, :, :side], mat_own[1::2, :, :side], (2, 4))
        right = chip_scatter(mat_own[:2, :, side:], mat_own[2:, :, side:], (4, 2))
        mat_sum = jnp.concatenate([left, right], axis=1)
    else:
        mat_sum = chip_scatter(mat_own, None, None)
    mat_sum = tp_scatter(
        [mat_sum[:, r * heads_tp : (r + 1) * heads_tp] for r in range(tp_count)], 1
    )
    mat_own = pick(mat_sum[:shard], mat_sum[shard:])
    mat_away = swap_fsdp(pick(mat_sum[shard:], mat_sum[:shard]), 1)
    query_mat_sum = pick(mat_own, mat_away)
    out_mat_sum = pick(mat_away, mat_own).T

    features = jnp.stack(
        [
            jnp.sum(norm_one_grad * normal, axis=0),
            jnp.sum(norm_one_grad, axis=0),
            ffn_vectors[0, :width],
            ffn_vectors[1, :width],
            jnp.sum(cotangent.astype(F32), axis=0),
        ]
    )
    wide = lambda value: jnp.pad(value, ((0, 0), (0, 0), (0, 128 - value.shape[2])))
    features = wide(features.reshape(5, fsdp_count, shard).swapaxes(0, 1))
    query_sums = jnp.sum(query_low.astype(F32), axis=0).reshape(tp_count, -1)
    up_sums = core_order(up_shift_grad, jnp.zeros_like(up_shift_grad), axis=1)
    up_sums = jnp.stack([up_sums, jnp.zeros_like(up_sums)], axis=1).reshape(tp_count, -1)
    along = relative(jnp.concatenate([query_sums, up_sums], axis=1), 0, "tp")
    query_sums = along[:, :heads_tp].reshape(tp_count, fsdp_count, -1).swapaxes(0, 1)
    up_sums = along[:, heads_tp:].reshape(tp_count, fsdp_count, -1).swapaxes(0, 1)
    kv_sums = jnp.sum(kv_low_grad.astype(F32), axis=0).reshape(fsdp_count, 1, -1)
    vectors = jnp.concatenate(
        [
            grad_kv_mat.reshape(fsdp_count, shard, -1),
            features,
            wide(query_sums),
            wide(up_sums),
            wide(kv_sums),
        ],
        axis=1,
    )
    vectors = relative(vectors.reshape(chips, -1), 0, "fsdp").reshape(vectors.shape)
    lines = vectors.shape[1]
    vectors = vectors.reshape(chips, 2, lines, 128)
    vectors = pick(vectors[:, 0], vectors[:, 1]) + swap_fsdp(pick(vectors[:, 1], vectors[:, 0]), 1)
    for bit in reversed(bits_of(fsdp_count)[1:]):
        half = vectors.shape[0] // 2
        vectors = vectors[:half] + swap_fsdp(vectors[half:], bit)
    for bit in bits_of(tp_count):
        vectors = vectors + swap_tp(vectors, bit)
    output, input_grad = finish(
        *(part_kept, part_core, part_tp, tokens, cotangent, attended_out),
        *(norm_one_grad, gain_one, gain_two, out_shift + down_shift),
    )
    vectors = vectors[0]
    features = vectors[shard : shard + 5, :shard]
    tail = vectors[shard + 5 :]
    query_bias_sum = lax.dynamic_slice_in_dim(tail, rank, 1, 0)[:, : query_bias.shape[1]]
    up_bias_sum = lax.dynamic_slice_in_dim(tail, tp_count + rank, 1, 0)[:, : up_bias.shape[1]]
    return (
        output,
        key_cache,
        input_grad,
        features[0],
        features[1],
        features[2],
        features[3],
        query_mat_sum,
        query_bias_sum,
        vectors[:shard],
        tail[2 * tp_count, : kv_bias.shape[0]],
        out_mat_sum,
        features[4],
        up_mat_sum,
        up_bias_sum,
        down_mat_sum,
        features[4],
    )


def solution(mesh):
    rows = P(("fsdp", "tp"), None)
    one = P("fsdp")
    tall = P("fsdp", "tp")
    turned = P("tp", "fsdp")
    lone = P("fsdp", None)
    return jax.shard_map(
        body,
        mesh=mesh,
        in_specs=(
            *(rows, rows, one, lone, one, one, one, one, tall, turned),
            *(lone, one, turned, one, tall, turned, turned, one),
        ),
        out_specs=(
            *(rows, rows, rows, one, one, one, one, tall, turned),
            *(lone, one, turned, one, tall, turned, turned, one),
        ),
        check_vma=False,
    )
```

```python
import math

import jax
import jax.numpy as jnp
from jax import lax
from jax.experimental import pallas as pl
from jax.experimental.pallas import tpu as pltpu
from jax.sharding import PartitionSpec as P


HD = 64
ROT = 16
BLK = 128
TRUNK = 8
FIRST_LEAF = 10
TILE = 64
HEADS_STEP = 12
NORM_EPS = 1e-05
MASKED = -1000000000.0
BF = jnp.bfloat16
F32 = jnp.float32


def dot(left, right, left_dim, right_dim):
    return lax.dot_general(
        left, right, (((left_dim,), (right_dim,)), ((), ())), preferred_element_type=F32
    )


def add_low(left, right):
    return (left.astype(F32) + right.astype(F32)).astype(BF)


def swap(value, axis, bit):
    count = lax.axis_size(axis)
    return lax.ppermute(value, axis, [(i, i ^ bit) for i in range(count)])


def swap_fsdp(value, bit):
    return swap(value, "fsdp", bit)


def swap_tp(value, bit):
    return swap(value, "tp", bit)


def bits_of(count):
    return [1 << k for k in range(count.bit_length() - 1)]


def core_order(mine, other, axis=0):
    core = lax.axis_index("fsdp") & 1
    return jnp.where(
        core == 0,
        jnp.concatenate([mine, other], axis=axis),
        jnp.concatenate([other, mine], axis=axis),
    )


def direct(count):
    return count == 8


def chip_gather(value):
    count = lax.axis_size("fsdp")
    if direct(count):
        return [value] + [swap_fsdp(value, bit) for bit in (2, 4, 6)]
    for bit in bits_of(count)[1:]:
        value = jnp.concatenate([value, swap_fsdp(value, bit)], axis=0)
    return [relative(value, 0, "fsdp")]


def chip_scatter(kept, sent, bits):
    value = kept
    if sent is None:
        value = relative(kept.reshape(-1, kept.shape[2]), 0, "fsdp")
        bits = bits_of(lax.axis_size("fsdp"))[:0:-1]
        value = value.reshape(bits[0], -1, kept.shape[2])
    else:
        taken = swap_fsdp(sent, bits[0])
        value = add_low(kept, taken)
        bits = bits[1:]
    for bit in bits:
        half = value.shape[0] // 2
        value = add_low(value[:half], swap_fsdp(value[half:], bit))
    return value[0]


def tp_gather(value, axis):
    count = lax.axis_size("tp")
    pieces = {0: value}
    for bit in reversed(bits_of(count)):
        order = sorted(pieces)
        sent = [pieces[r] for r in order]
        taken = swap_tp(sent[0] if len(sent) == 1 else jnp.concatenate(sent, axis=axis), bit)
        size = taken.shape[axis] // len(order)
        for place, r in enumerate(order):
            pieces[r | bit] = lax.slice_in_dim(taken, place * size, (place + 1) * size, axis=axis)
    return [pieces[r] for r in range(count)]


def tp_scatter_direct(pieces):
    total = pieces[0].astype(F32)
    for r in range(1, len(pieces)):
        total = total + swap_tp(pieces[r].astype(BF), r).astype(F32)
    return total


def tp_scatter_even(value, size):
    count = value.shape[1] // size // 2
    blocks = [value[:, k * size : (k + 1) * size] for k in range(2 * count)]
    ups, downs = blocks[:count], blocks[count:]
    for bit in reversed(bits_of(lax.axis_size("tp"))[1:]):
        count //= 2
        taken = swap_tp(jnp.concatenate(ups[count:] + downs[count:], axis=1), bit)
        taken = [taken[:, k * size : (k + 1) * size].astype(F32) for k in range(2 * count)]
        ups = [ups[k].astype(F32) + taken[k] for k in range(count)]
        downs = [downs[k].astype(F32) + taken[count + k] for k in range(count)]
    return jnp.concatenate(ups + downs, axis=1)


def relative(value, axis, name):
    count = lax.axis_size(name)
    index = lax.axis_index(name)
    if name == "fsdp":
        count, index = count // 2, index // 2
    size = value.shape[axis] // count
    blocks = [lax.slice_in_dim(value, k * size, (k + 1) * size, axis=axis) for k in range(count)]
    for bit in bits_of(count):
        taken = (index & bit) != 0
        blocks = [jnp.where(taken, blocks[k ^ bit], blocks[k]) for k in range(count)]
    return jnp.concatenate(blocks, axis=axis)


def attention_kernel(first, *refs):
    (
        meta_ref,
        query_ref,
        grad_ref,
        kv_ref,
        cos_ref,
        back_ref,
        ahead_ref,
    ) = refs[:7]
    refs = refs[7:]
    earlier = None
    if first:
        earlier = refs[2]
        refs = refs[3:]
    (
        attended_ref,
        query_grad_ref,
        kv_grad_ref,
        queries,
        grads,
        outs,
        query_grads,
        keys,
        values,
        acc,
        bias,
    ) = refs
    step = pl.program_id(0)
    pair_count = query_ref.shape[1] // 128
    groups = queries.shape[0]
    trunk = TRUNK * BLK
    block = meta_ref[step + first, 0]
    offset = meta_ref[step + first, 1]
    parent = meta_ref[step + first, 2]

    @pl.when(step == 0)
    def _():
        if earlier is None:
            kv_grad_ref[...] = jnp.zeros_like(kv_grad_ref)
        else:
            kv_grad_ref[...] = earlier[...]
        keys[:trunk, :] = kv_ref[:trunk, :HD]
        values[:trunk, :] = kv_ref[:trunk, HD:]

    parent_rows = pl.ds(pl.multiple_of(parent * BLK, BLK), BLK)
    own_rows = pl.ds(pl.multiple_of(block * BLK, BLK), BLK)
    keys[trunk : trunk + BLK, :] = kv_ref[parent_rows, :HD]
    values[trunk : trunk + BLK, :] = kv_ref[parent_rows, HD:]
    keys[trunk + BLK :, :] = kv_ref[own_rows, :HD]
    values[trunk + BLK :, :] = kv_ref[own_rows, HD:]

    row = lax.broadcasted_iota(jnp.int32, bias.shape, 0) + offset
    col = lax.broadcasted_iota(jnp.int32, bias.shape, 1)
    in_trunk = block < TRUNK
    trunk_limit = jnp.where(in_trunk, block * BLK + row, trunk)
    own_limit = jnp.where(in_trunk, -1, row)
    is_leaf = (block >= FIRST_LEAF).astype(jnp.int32)
    parent_limit = is_leaf * (2 * trunk) - 1
    limit = jnp.where(
        col < trunk, trunk_limit, jnp.where(col < trunk + BLK, parent_limit, own_limit + trunk + BLK)
    )
    bias[...] = jnp.where(col <= limit, 0.0, MASKED)

    cos = cos_ref[...]
    back = back_ref[...]
    ahead = ahead_ref[...]
    per_group = HEADS_STEP // 2
    for pair in range(pair_count):
        lanes = slice(pair * 128, (pair + 1) * 128)
        linear = query_ref[:, lanes]
        turned = (
            linear * cos
            + pltpu.roll(linear, 128 - ROT // 2, 1) * back
            + pltpu.roll(linear, ROT // 2, 1) * ahead
        ).astype(BF) * jnp.asarray(1.0 / math.sqrt(HD), BF)
        grad = grad_ref[:, lanes]
        group, place = divmod(pair, per_group)
        for side in range(2):
            rows = slice((2 * place + side) * TILE, (2 * place + side + 1) * TILE)
            queries[group, rows, :] = turned[:, side * HD : (side + 1) * HD]
            grads[group, rows, :] = grad[:, side * HD : (side + 1) * HD]

    acc[...] = jnp.zeros_like(acc)

    def one_group(group, carry):
        query = queries[group]
        grad = grads[group]
        key = keys[...]
        value = values[...]
        score = dot(query, key, 1, 1)
        score = (score.reshape(HEADS_STEP, TILE, -1) + bias[...][None]).reshape(score.shape)
        peak = jnp.max(score, axis=1, keepdims=True)
        exponent = jnp.exp(score - peak)
        total = jnp.sum(exponent, axis=1, keepdims=True)
        prob = exponent * (1.0 / total)
        prob_low = prob.astype(BF)
        outs[group] = dot(prob_low, value, 1, 0)
        grad_prob = dot(grad, value, 1, 1)
        delta = jnp.sum(prob * grad_prob, axis=1, keepdims=True)
        score_grad = (prob * (grad_prob - delta)).astype(BF)
        query_grads[group] = dot(score_grad, key, 1, 0)
        acc[:HD, :] += dot(query, score_grad, 0, 0)
        acc[HD:, :] += dot(grad, prob_low, 0, 0)
        return carry

    lax.fori_loop(0, groups, one_group, 0)

    scale = 1.0 / math.sqrt(HD)
    for pair in range(pair_count):
        lanes = slice(pair * 128, (pair + 1) * 128)
        group, place = divmod(pair, per_group)
        first = slice(2 * place * TILE, (2 * place + 1) * TILE)
        second = slice((2 * place + 1) * TILE, (2 * place + 2) * TILE)
        attended_ref[:, lanes] = jnp.concatenate(
            [outs[group, first, :], outs[group, second, :]], axis=1
        ).astype(BF)
        turned = scale * jnp.concatenate(
            [query_grads[group, first, :], query_grads[group, second, :]], axis=1
        )
        query_grad_ref[:, lanes] = (
            turned * cos
            - pltpu.roll(turned, 128 - ROT // 2, 1) * back
            - pltpu.roll(turned, ROT // 2, 1) * ahead
        ).astype(BF)
    kv_grad_ref[:, :trunk] += acc[:, :trunk]
    kv_grad_ref[:, parent_rows] += acc[:, trunk : trunk + BLK]
    kv_grad_ref[:, own_rows] += acc[:, trunk + BLK :]


def attention(meta, query_lin, grad_attended, key_value, cos, back, ahead, first, last, earlier):
    rows, width = query_lin.shape
    groups = width // HD // HEADS_STEP
    seen = (TRUNK + 2) * BLK
    stacked = HEADS_STEP * TILE
    tile = lambda lanes: pl.BlockSpec((TILE, lanes), lambda i, m: (i + first, 0))
    whole = pl.BlockSpec(key_value.shape, lambda i, m: (0, 0))
    anywhere = pl.BlockSpec(memory_space=pl.ANY)
    turned = pl.BlockSpec(key_value.shape[::-1], lambda i, m: (0, 0))
    given = [] if earlier is None else [anywhere, anywhere, turned]
    count = last - first
    work = 6 * count * TILE * (width // HD) * seen
    return pl.pallas_call(
        lambda *refs: attention_kernel(first, *refs),
        out_shape=(
            jax.ShapeDtypeStruct((rows, width), BF),
            jax.ShapeDtypeStruct((rows, width), BF),
            jax.ShapeDtypeStruct(key_value.shape[::-1], F32),
        ),
        grid_spec=pltpu.PrefetchScalarGridSpec(
            num_scalar_prefetch=1,
            grid=(count,),
            in_specs=[tile(width), tile(width), whole, tile(128), tile(128), tile(128)] + given,
            out_specs=[tile(width), tile(width), turned],
            scratch_shapes=[
                pltpu.VMEM((groups, stacked, HD), BF),
                pltpu.VMEM((groups, stacked, HD), BF),
                pltpu.VMEM((groups, stacked, HD), F32),
                pltpu.VMEM((groups, stacked, HD), F32),
                pltpu.VMEM((seen, HD), BF),
                pltpu.VMEM((seen, HD), BF),
                pltpu.VMEM((2 * HD, seen), F32),
                pltpu.VMEM((TILE, seen), F32),
            ],
        ),
        input_output_aliases={} if earlier is None else {7: 0, 8: 1},
        cost_estimate=pl.CostEstimate(
            flops=2 * 256 * work, bytes_accessed=2 * rows * width, transcendentals=work // 6
        ),
        compiler_params=pltpu.CompilerParams(vmem_limit_bytes=36 * 2**20),
    )(meta, query_lin, grad_attended, key_value, cos, back, ahead, *(earlier or ()))


def local_kernel(kernel, outs, args, scratch=(), flops=0, scalars=1, mib=56):
    return pl.pallas_call(
        kernel,
        out_shape=[jax.ShapeDtypeStruct(shape, kind) for shape, kind in outs],
        in_specs=[pl.BlockSpec(memory_space=pltpu.SMEM)] * scalars
        + [pl.BlockSpec(memory_space=pltpu.VMEM)] * (len(args) - scalars),
        out_specs=[pl.BlockSpec(memory_space=pltpu.VMEM)] * len(outs),
        scratch_shapes=list(scratch),
        cost_estimate=pl.CostEstimate(flops=flops, bytes_accessed=2**20, transcendentals=0),
        compiler_params=pltpu.CompilerParams(vmem_limit_bytes=mib * 2**20),
    )(*args)


def identity(size):
    row = lax.broadcasted_iota(jnp.int32, (size, size), 0)
    col = lax.broadcasted_iota(jnp.int32, (size, size), 1)
    return jnp.where(row == col, 1.0, 0.0).astype(BF)


LINES = 16


def pack_kernel(place, query, out, up, down, kv, *refs):
    lines = refs[:-4]
    kept, sent, small, buffer = refs[-4:]
    core = place[0]
    shard, heads = query.shape
    half = up.shape[1] // 2
    unit = identity(shard)
    out_turned = dot(unit, out[...], 1, 1).astype(BF)
    down_turned = down[...]
    first = core == 0

    def pair(one, two, at):
        size = one.shape[1]
        one, two = one.astype(F32), two.astype(F32)
        kept[:, at : at + size] = jnp.where(first, one, two).astype(BF)
        sent[:, at : at + size] = jnp.where(first, two, one).astype(BF)

    pair(query[...], out_turned, 0)
    pair(up[:, :half], up[:, half:], heads)
    pair(down_turned[:, :half], down_turned[:, half:], heads + half)
    buffer[...] = jnp.zeros_like(buffer)
    for k, line in enumerate(lines):
        buffer[k : k + 1, : line.shape[1]] = line[...].astype(F32)
    small[:LINES, :] = buffer[...].astype(BF)
    small[LINES:, :] = kv[...]


def block_at(chip, k, size):
    return pl.ds(pl.multiple_of((chip ^ k) * size, size), size)


def place_kernel(place, *refs):
    out = refs[-1]
    for k, ref in enumerate(refs[:-1]):
        out[block_at(place[1], k, ref.shape[0]), :] = ref[...]


def send_order(bits):
    order = [0]
    for bit in reversed(bits):
        order = order + [k | bit for k in order]
    return order


def put_blocks(chip, source, kept, sent, bits):
    count = kept.shape[0] + (sent.shape[0] if sent is not None else 0)
    size = kept.shape[1]
    order = send_order(bits) if sent is not None else [0]
    for spot, k in enumerate(order):
        rows = block_at(chip, k, size) if count > 1 else slice(None)
        value = source[rows, :].astype(BF)
        if spot < kept.shape[0]:
            kept[spot] = value
        else:
            sent[spot - kept.shape[0]] = value


def finish_kernel(
    kept, taken, from_pair, tokens, grad, base, one_grad, gain_one, gain_two, shift, out, input_grad
):
    part = kept[:, 0].astype(F32) + taken[:, 0].astype(F32) + from_pair[:, 0].astype(F32)
    value = tokens[...].astype(F32)
    out[...] = (value + base[...] + shift[...] + part[0]).astype(BF)
    centred = value - jnp.mean(value, axis=1, keepdims=True)
    inverse = lax.rsqrt(jnp.mean(centred * centred, axis=1, keepdims=True) + NORM_EPS)
    normal = centred * inverse
    scaled = one_grad[...] * gain_one[...] + part[1] * gain_two[...]
    mean = jnp.mean(scaled, axis=1, keepdims=True)
    along = jnp.mean(scaled * normal, axis=1, keepdims=True)
    input_grad[...] = (
        grad[...].astype(F32) + inverse * (scaled - mean - normal * along)
    ).astype(BF)


def finish(kept, taken, from_pair, tokens, grad, base, one_grad, gain_one, gain_two, shift):
    rows, width = tokens.shape
    half = kept.shape[2]
    parts = pl.BlockSpec((2, 1, half, width), lambda i: (0, i, 0, 0))
    tile = pl.BlockSpec((half, width), lambda i: (i, 0))
    line = pl.BlockSpec((1, width), lambda i: (0, 0))
    call = pl.pallas_call(
        finish_kernel,
        grid=(rows // half,),
        out_shape=[jax.ShapeDtypeStruct((rows, width), BF)] * 2,
        in_specs=[parts] * 3 + [tile] * 4 + [line] * 3,
        out_specs=[tile] * 2,
        cost_estimate=pl.CostEstimate(
            flops=30 * rows * width, bytes_accessed=24 * rows * width, transcendentals=0
        ),
        name="finish",
    )
    return call(
        kept, taken, from_pair, tokens, grad, base, one_grad, gain_one, gain_two, shift
    )


def mat_grad_kernel(place, one, query_low, grad, attended, kept, sent, first, second):
    core = place[0]
    first[...] = dot(one[...], query_low[...], 0, 0)
    second[...] = dot(grad[...], attended[...], 0, 0)
    count, size = kept.shape[:2]
    for k in range(count):
        rows = block_at(place[1], k, size) if count > 1 else slice(None)
        here, there = first[rows, :], second[rows, :]
        kept[k] = jnp.where(core == 0, here, there).astype(BF)
        sent[k] = jnp.where(core == 0, there, here).astype(BF)


def ffn_kernel(weight_count, sending, *refs):
    place, gain, shift, up_shift = refs[:4]
    token_refs, grad_refs = refs[4:8], refs[8:12]
    weights = refs[12 : 12 + weight_count]
    refs = refs[12 + weight_count :]
    kept, sent, sums = refs[:3]
    up_kept, down_kept = refs[3:5]
    up_sent, down_sent = refs[5:7] if sending else (None, None)
    tokens, grads, up, down, two_all, low_all, act_all, total = refs[7 if sending else 5 :]
    hidden_own = up.shape[1]
    tile = tokens.shape[1]
    pieces = tokens.shape[0]
    for k in range(4):
        for side in range(2):
            tokens[2 * k + side] = token_refs[k][side * tile : (side + 1) * tile, :]
            grads[2 * k + side] = grad_refs[k][side * tile : (side + 1) * tile, :]
    for k, ref in enumerate(weights):
        rows = block_at(place[1], k, ref.shape[0]) if weight_count > 1 else slice(None)
        up[rows, :] = ref[:, :hidden_own]
        down[rows, :] = ref[:, hidden_own:]
    sums[...] = jnp.zeros_like(sums)

    def one_tile(i, carry):
        value = tokens[i].astype(F32)
        centred = value - jnp.mean(value, axis=1, keepdims=True)
        variance = jnp.mean(centred * centred, axis=1, keepdims=True)
        normal = centred * lax.rsqrt(variance + NORM_EPS)
        two = (normal * gain[...] + shift[...]).astype(BF)
        hidden = dot(two, up[...], 1, 0) + up_shift[...]
        below = 0.5 * (1.0 + lax.erf(hidden * (1.0 / math.sqrt(2.0))))
        active = (hidden * below).astype(BF)
        bell = jnp.exp(-0.5 * hidden * hidden) * (1.0 / math.sqrt(2.0 * math.pi))
        grad = grads[i]
        slope_grad = dot(grad, down[...], 1, 0) * (below + hidden * bell)
        low = slope_grad.astype(BF)
        branch = dot(active, down[...], 1, 1)
        norm_grad = dot(low, up[...], 1, 1)
        rows = pl.ds(pl.multiple_of(i * tile, tile), tile)
        two_all[rows, :] = two
        low_all[rows, :] = low
        act_all[rows, :] = active
        sums[0:1, :] += jnp.sum(norm_grad * normal, axis=0, keepdims=True)
        sums[1:2, :] += jnp.sum(norm_grad, axis=0, keepdims=True)
        sums[2:3, :hidden_own] += jnp.sum(low.astype(F32), axis=0, keepdims=True)
        branch = branch.astype(BF)
        norm_grad = norm_grad.astype(BF)

        @pl.when(i < pieces // 2)
        def _():
            kept[0, i] = branch
            kept[1, i] = norm_grad

        @pl.when(i >= pieces // 2)
        def _():
            sent[0, i - pieces // 2] = branch
            sent[1, i - pieces // 2] = norm_grad

        return carry

    lax.fori_loop(0, pieces, one_tile, 0)
    total[...] = dot(two_all[...], low_all[...], 0, 0)
    put_blocks(place[1], total, up_kept, up_sent, (1, 2))
    flat = grads[...].reshape(act_all.shape[0], -1)
    total[...] = dot(flat, act_all[...], 0, 0)
    put_blocks(place[1], total, down_kept, down_sent, (2, 1))


def tree_tables(block_segment, segment_path, rank, rows):
    blocks = block_segment.shape[0]
    seg_count = segment_path.shape[1]
    one_hot = (block_segment[:, None] == jnp.arange(seg_count)[None, :]).astype(F32)
    linked = jnp.dot(jnp.dot(one_hot, segment_path.astype(F32)), one_hot.T)
    order = jnp.arange(blocks)
    before = jnp.sum(jnp.where(order[:, None] > order[None, :], linked, 0.0), axis=1)
    first_row = rank * rows
    row = first_row + jnp.arange(rows, dtype=jnp.int32)
    own = (row[:, None] // BLK == order[None, :]).astype(F32)
    position = jnp.sum(own * before[None, :], axis=1) * BLK + (row % BLK).astype(F32)
    start = first_row + TILE * jnp.arange(rows // TILE, dtype=jnp.int32)
    block = start // BLK
    second = jnp.sum((block[:, None] == order[None, :]) * linked[None, :, TRUNK + 1], axis=1)
    parent = jnp.where((block >= FIRST_LEAF) & (second > 0.5), TRUNK + 1, TRUNK)
    meta = jnp.stack([block, start % BLK, parent], axis=1).astype(jnp.int32)
    return position, meta


def body(
    tokens,
    cotangent,
    block_segment,
    segment_path,
    norm1_gain,
    norm1_bias,
    norm2_gain,
    norm2_bias,
    query_weight,
    query_bias,
    kv_weight,
    kv_bias,
    out_weight,
    out_bias,
    up_weight,
    up_bias,
    down_weight,
    down_bias,
):
    fsdp_count = lax.axis_size("fsdp")
    tp_count = lax.axis_size("tp")
    chips = fsdp_count // 2
    core = lax.axis_index("fsdp") & 1
    rank = lax.axis_index("tp")
    rows, width = tokens.shape
    shard = norm1_gain.shape[0]
    hidden_half = up_weight.shape[1] // 2
    heads_tp = query_weight.shape[1]
    chip = lax.axis_index("fsdp") // 2
    blocks = chips if direct(fsdp_count) else 1
    place = jnp.stack([core, chip]).astype(jnp.int32)
    pick = lambda first, second: jnp.where(core == 0, first, second)

    lines = [norm1_gain, norm1_bias, norm2_gain, norm2_bias, out_bias, down_bias, kv_bias]
    lines = [line[None, :] for line in lines] + [query_bias, up_bias]
    packed = heads_tp + 2 * hidden_half
    kept, sent, small = local_kernel(
        pack_kernel,
        [((shard, packed), BF), ((shard, packed), BF), ((LINES + shard, 128), BF)],
        [place, query_weight, out_weight, up_weight, down_weight.T, kv_weight, *lines],
        [pltpu.VMEM((LINES, 128), F32)],
    )
    small = small[None]
    small = core_order(small, swap_fsdp(small, 1))
    piece = core_order(kept, swap_fsdp(sent, 1))
    grad_core = swap_fsdp(cotangent, 1)
    tokens_core = swap_fsdp(tokens, 1)
    mat_piece = jnp.concatenate(tp_gather(piece[:, :heads_tp], 1), axis=1)
    mat_pieces = chip_gather(mat_piece)
    if blocks > 1:
        mat_kept = local_kernel(place_kernel, [((width, width), BF)], [place, *mat_pieces])[0]
    else:
        mat_kept = mat_pieces[0]
    mat_other = swap_fsdp(mat_kept, 1)
    query_mat = pick(mat_kept, mat_other)
    out_mat = pick(mat_other, mat_kept)

    for bit in bits_of(fsdp_count)[1:]:
        small = jnp.concatenate([small, swap_fsdp(small, bit)], axis=0)
    small = relative(small.reshape(chips, -1), 0, "fsdp").reshape(small.shape)
    kv_mat = small[:, LINES:].reshape(width, -1)
    line_at = lambda k, size: small[:, k, :size].reshape(1, -1)
    gain_one, shift_one, gain_two, shift_two, out_shift, down_shift = (
        line_at(k, shard).astype(F32) for k in range(6)
    )
    kv_shift = line_at(6, kv_bias.shape[0]).astype(F32)
    query_own = line_at(7, query_bias.shape[1])
    up_own = line_at(8, up_bias.shape[1])
    up_own = pick(up_own[:, :hidden_half], up_own[:, hidden_half:])
    shift_own = jnp.concatenate([query_own, up_own], axis=1)
    shift_size = shift_own.shape[1]
    shift_own = jnp.pad(shift_own, ((0, 0), (0, -shift_size % 2048))).reshape(-1, 128)

    inputs = tokens.astype(F32)
    centred = inputs - jnp.mean(inputs, axis=-1, keepdims=True)
    inverse = lax.rsqrt(jnp.mean(centred * centred, axis=-1, keepdims=True) + NORM_EPS)
    normal = centred * inverse
    low_one = (normal * gain_one + shift_one).astype(BF)

    ffn_piece, tokens_sent, grad_sent, _ = lax.optimization_barrier(
        (piece[:, heads_tp:], tokens, cotangent, mat_piece)
    )
    ups = [ffn_piece[:, :hidden_half]]
    downs = [ffn_piece[:, hidden_half:]]
    for bit in bits_of(tp_count)[1:]:
        near = swap_tp(jnp.concatenate(ups + downs, axis=1), bit)
        near = [near[:, k * hidden_half : (k + 1) * hidden_half] for k in range(2 * len(ups))]
        ups, downs = ups + near[: len(ups)], downs + near[len(ups) :]
    ffn_piece = jnp.concatenate(ups + downs, axis=1)
    ffn_piece, mat_pieces[-1] = lax.optimization_barrier((ffn_piece, mat_pieces[-1]))
    ffn_pieces = chip_gather(ffn_piece)
    hidden_own = hidden_half * tp_count // 2
    tokens_tp = swap_tp(tokens_sent, 1)
    grad_tp = swap_tp(grad_sent, 1)

    position, meta = tree_tables(block_segment, segment_path, rank, rows)
    lane = jnp.arange(128, dtype=jnp.int32)
    frequency = jnp.exp((lane % (ROT // 2)).astype(F32) * (-2.0 * math.log(10000.0) / ROT))
    phase = position[:, None] * frequency[None, :]
    cos_wave = jnp.cos(phase)
    sin_wave = jnp.sin(phase)
    in_head = lane % HD
    cos = jnp.where(in_head < ROT, cos_wave, 1.0)
    back = jnp.where(in_head < ROT // 2, -sin_wave, 0.0)
    ahead = jnp.where((in_head >= ROT // 2) & (in_head < ROT), sin_wave, 0.0)
    is_key = lane < HD
    cos_key = jnp.where(is_key, cos, 1.0)
    back_key = jnp.where(is_key, back, 0.0)
    ahead_key = jnp.where(is_key, ahead, 0.0)

    kv_lin = dot(low_one, kv_mat, 1, 0) + kv_shift
    key_cache = (
        kv_lin * cos_key
        + jnp.roll(kv_lin, -(ROT // 2), 1) * back_key
        + jnp.roll(kv_lin, ROT // 2, 1) * ahead_key
    ).astype(BF)
    gathered = tp_gather(jnp.concatenate([key_cache, shift_own], axis=0), 0)
    kv_all = relative(jnp.concatenate([g[:rows] for g in gathered], axis=0), 0, "tp")
    shifts = jnp.concatenate(
        [g[rows:].reshape(1, -1)[:, :shift_size] for g in gathered], axis=0
    ).astype(F32)
    query_shift = shifts[:, :heads_tp].reshape(-1)
    up_shift = shifts[::2, heads_tp:].reshape(1, -1)

    query_lin = dot(low_one, query_mat, 1, 0) + query_shift
    grad_attended = dot(cotangent, out_mat, 1, 0).astype(BF)
    tiles = rows // TILE
    middle = tiles * 5 // 7
    operands = (meta, query_lin, grad_attended, kv_all, cos, back, ahead)
    earlier = attention(*operands, 0, middle, None)
    tokens_tp, grad_tp, *earlier = lax.optimization_barrier((tokens_tp, grad_tp, *earlier))
    tokens_far = swap_fsdp(tokens_tp, 1)
    grad_far = swap_fsdp(grad_tp, 1)
    attended, query_low, kv_grad = attention(*operands, middle, tiles, tuple(earlier))

    first_token, attended, query_low, kv_grad = lax.optimization_barrier(
        (tokens, attended, query_low, kv_grad)
    )
    half = rows // 2
    block_rows = width // blocks
    halves = [((2, 4, half, width), BF)] * 2 + [((8, max(width, hidden_own)), F32)]
    grad_kept = [((max(blocks // 2, 1), block_rows, hidden_own), BF)] * 2
    grad_sent = grad_kept if blocks > 1 else []
    ffn_out = local_kernel(
        lambda *refs: ffn_kernel(len(ffn_pieces), blocks > 1, *refs),
        halves + grad_kept + grad_sent,
        [
            *(place, gain_two, shift_two, up_shift),
            *(first_token, tokens_tp, tokens_core, tokens_far),
            *(cotangent, grad_tp, grad_core, grad_far),
            *ffn_pieces,
        ],
        [
            pltpu.VMEM((8, half, width), BF),
            pltpu.VMEM((8, half, width), BF),
            pltpu.VMEM((width, hidden_own), BF),
            pltpu.VMEM((width, hidden_own), BF),
            pltpu.VMEM((4 * rows, width), BF),
            pltpu.VMEM((4 * rows, hidden_own), BF),
            pltpu.VMEM((4 * rows, hidden_own), BF),
            pltpu.VMEM((width, hidden_own), F32),
        ],
        mib=56,
        flops=12 * 4 * rows * width * hidden_own,
    )
    part_kept, part_sent, ffn_vectors, up_kept, down_kept = ffn_out[:5]
    up_sent, down_sent = ffn_out[5:] if blocks > 1 else (None, None)
    part_core = swap_fsdp(part_sent, 1)
    part_tp = swap_tp(add_low(part_kept[:, 2:], part_core[:, 2:]), 1)
    up_sum = chip_scatter(up_kept, up_sent, (2, 4))
    down_sum = chip_scatter(down_kept, down_sent, (4, 2))
    ffn_sum = tp_scatter_even(jnp.concatenate([up_sum, down_sum], axis=1), hidden_half)
    ffn_own = pick(ffn_sum[:shard], ffn_sum[shard:])
    ffn_other = swap_fsdp(pick(ffn_sum[shard:], ffn_sum[:shard]), 1)
    up_mat_sum = core_order(ffn_own[:, :hidden_half], ffn_other[:, :hidden_half], axis=1)
    down_mat_sum = core_order(ffn_own[:, hidden_half:], ffn_other[:, hidden_half:], axis=1).T
    up_shift_grad = ffn_vectors[2, :hidden_own].reshape(-1, hidden_half)

    attended_out = dot(attended, out_mat, 1, 1)
    kv_pieces = relative(kv_grad.T, 0, "tp").reshape(tp_count, rows, -1)
    kv_sum = tp_scatter_direct([kv_pieces[r] for r in range(tp_count)])
    kv_low_grad = (
        kv_sum * cos_key
        - jnp.roll(kv_sum, -(ROT // 2), 1) * back_key
        - jnp.roll(kv_sum, ROT // 2, 1) * ahead_key
    ).astype(BF)
    mat_own, mat_given = local_kernel(
        mat_grad_kernel,
        [((blocks, block_rows, width), BF)] * 2,
        [place, low_one, query_low, cotangent, attended],
        [pltpu.VMEM((width, width), F32)] * 2,
        mib=56,
        flops=4 * rows * width * width,
    )
    grad_kv_mat = dot(low_one, kv_low_grad, 0, 0)
    norm_one_grad = dot(query_low, query_mat, 1, 1) + dot(kv_low_grad, kv_mat, 1, 1)
    mat_given = swap_fsdp(mat_given, 1)
    mat_own = add_low(mat_own, mat_given)
    if blocks > 1:
        side = width // 2
        left = chip_scatter(mat_own[::2, :, :side], mat_own[1::2, :, :side], (2, 4))
        right = chip_scatter(mat_own[:2, :, side:], mat_own[2:, :, side:], (4, 2))
        mat_sum = jnp.concatenate([left, right], axis=1)
    else:
        mat_sum = chip_scatter(mat_own, None, None)
    mat_sum = tp_scatter_direct(
        [mat_sum[:, r * heads_tp : (r + 1) * heads_tp] for r in range(tp_count)]
    )
    mat_own = pick(mat_sum[:shard], mat_sum[shard:])
    mat_away = swap_fsdp(pick(mat_sum[shard:], mat_sum[:shard]), 1)
    query_mat_sum = pick(mat_own, mat_away)
    out_mat_sum = pick(mat_away, mat_own).T

    features = jnp.stack(
        [
            jnp.sum(norm_one_grad * normal, axis=0),
            jnp.sum(norm_one_grad, axis=0),
            ffn_vectors[0, :width],
            ffn_vectors[1, :width],
            jnp.sum(cotangent.astype(F32), axis=0),
        ]
    )
    wide = lambda value: jnp.pad(value, ((0, 0), (0, 0), (0, 128 - value.shape[2])))
    features = wide(features.reshape(5, fsdp_count, shard).swapaxes(0, 1))
    query_sums = jnp.sum(query_low.astype(F32), axis=0).reshape(tp_count, -1)
    up_sums = core_order(up_shift_grad, jnp.zeros_like(up_shift_grad), axis=1)
    up_sums = jnp.stack([up_sums, jnp.zeros_like(up_sums)], axis=1).reshape(tp_count, -1)
    along = relative(jnp.concatenate([query_sums, up_sums], axis=1), 0, "tp")
    query_sums = along[:, :heads_tp].reshape(tp_count, fsdp_count, -1).swapaxes(0, 1)
    up_sums = along[:, heads_tp:].reshape(tp_count, fsdp_count, -1).swapaxes(0, 1)
    kv_sums = jnp.sum(kv_low_grad.astype(F32), axis=0).reshape(fsdp_count, 1, -1)
    vectors = jnp.concatenate(
        [
            grad_kv_mat.reshape(fsdp_count, shard, -1),
            features,
            wide(query_sums),
            wide(up_sums),
            wide(kv_sums),
        ],
        axis=1,
    )
    vectors = relative(vectors.reshape(chips, -1), 0, "fsdp").reshape(vectors.shape)
    lines = vectors.shape[1]
    vectors = vectors.reshape(chips, 2, lines, 128)
    vectors = pick(vectors[:, 0], vectors[:, 1]) + swap_fsdp(pick(vectors[:, 1], vectors[:, 0]), 1)
    for bit in reversed(bits_of(fsdp_count)[1:]):
        half = vectors.shape[0] // 2
        vectors = vectors[:half] + swap_fsdp(vectors[half:], bit)
    vectors = vectors + sum(swap_tp(vectors, r) for r in range(1, tp_count))
    output, input_grad = finish(
        *(part_kept, part_core, part_tp, tokens, cotangent, attended_out),
        *(norm_one_grad, gain_one, gain_two, out_shift + down_shift),
    )
    vectors = vectors[0]
    features = vectors[shard : shard + 5, :shard]
    tail = vectors[shard + 5 :]
    query_bias_sum = lax.dynamic_slice_in_dim(tail, rank, 1, 0)[:, : query_bias.shape[1]]
    up_bias_sum = lax.dynamic_slice_in_dim(tail, tp_count + rank, 1, 0)[:, : up_bias.shape[1]]
    return (
        output,
        key_cache,
        input_grad,
        features[0],
        features[1],
        features[2],
        features[3],
        query_mat_sum,
        query_bias_sum,
        vectors[:shard],
        tail[2 * tp_count, : kv_bias.shape[0]],
        out_mat_sum,
        features[4],
        up_mat_sum,
        up_bias_sum,
        down_mat_sum,
        features[4],
    )


def solution(mesh):
    rows = P(("fsdp", "tp"), None)
    one = P("fsdp")
    tall = P("fsdp", "tp")
    turned = P("tp", "fsdp")
    lone = P("fsdp", None)
    return jax.shard_map(
        body,
        mesh=mesh,
        in_specs=(
            *(rows, rows, one, lone, one, one, one, one, tall, turned),
            *(lone, one, turned, one, tall, turned, turned, one),
        ),
        out_specs=(
            *(rows, rows, rows, one, one, one, one, tall, turned),
            *(lone, one, turned, one, tall, turned, turned, one),
        ),
        check_vma=False,
    )
```
